256 devices in a mesh: xy: 32 (over y_hi, z, core), gz: 8 (over y_lo, x).
Axes of the slice: x: 4, y: 4 (y_hi: 2, y_lo: 2; y = y_hi * 2 + y_lo), z: 8, core: 2. Of those that a mesh axis runs over, the one named last changes fastest.
Arguments:
- positions: float32 [3, 32, 6, 32, 128], P(None, 'xy', None, 'gz'), may hold values from 0 to 1
- cotangent: float32 [3, 32, 6, 32, 128], P(None, 'xy', None, 'gz'), may hold values from -6 to 6
- species: int32 [32, 6, 32, 128], P('xy', None, 'gz'), may hold values from 0 to 7
- counts: int32 [32, 6, 32], P('xy', None, 'gz'), may hold values from 8 to 128, as said below
- amplitude: float32 [8, 8], replicated, may hold values from 0.2 to 2
Outputs:
- position_cotangent: float32 [3, 32, 6, 32, 128], P(None, 'xy', None, 'gz')
- amplitude_grad: float32 [8, 8], replicated
The draws below stay inside these ranges and needn't reach their ends.
Inputs may be any that keep to these rules, and one draw needn't show every extreme that they name: The live beads of a cell fill its first counts slots; cell (0, 0, 0) holds 128 beads.
All inputs are finite; a program needn't handle non-finite values.
Results may differ from the reference program's by a relative error of at most 0.00021.
Values sent between devices are 32-bit elements; how exact they have to be, the bound alone decides.
No kernel may reach another device: no remote copies, remote signals or barrier semaphores. Data moves between devices by JAX's collectives and lax.ppermute only.
A program may use at most 64 MiB of HBM per device.

```python
import math
import jax
import jax.numpy as jnp
from jax import lax

CXD = 1
NYC = 6
SLOTS = 128
SPECIES = 8
NXC = 32
NZC = 32
NCELLS = 6144


def draw_counts(key, part):
    key_dense = jax.random.fold_in(key, 11)
    key_base = jax.random.fold_in(key, 12)
    column_blocks = NXC // CXD
    dense_block = jax.random.randint(key_dense, (column_blocks,), 0, 4) == 0
    dense_block = dense_block.at[0].set(True)
    factor = jnp.repeat(jnp.where(dense_block, 4, 1).astype(jnp.int32), CXD)
    base_count = jax.random.randint(key_base, (NXC, NYC, NZC), SLOTS // 16, SLOTS // 4 + 1)
    counts = jnp.minimum(factor[:, None, None] * base_count, SLOTS).astype(jnp.int32)
    return counts.at[0, 0, 0].set(SLOTS)


def with_ends(values, rng, smallest, high):
    spot = [jax.random.randint(jax.random.fold_in(rng, axis), (), 0, length) for axis, length in enumerate(values.shape)]
    widest = values.shape.index(max(values.shape))
    next_to = spot[:widest] + [(spot[widest] + 1) % values.shape[widest]] + spot[widest + 1:]
    return values.at[tuple(spot)].set(smallest).at[tuple(next_to)].set(high)


def block_scale(stream_key, dims, cuts, low, top_value):
    def one(dim, blocks):
        steps = jax.random.uniform(jax.random.fold_in(jax.random.fold_in(stream_key, 6), dim), (blocks,), jnp.float32, low / len(cuts), top_value / len(cuts))
        return jnp.repeat(jnp.exp(steps), dims[dim] // blocks).reshape((-1,) + (1,) * (len(dims) - dim - 1))

    gain = one(*cuts[0])
    for cut in cuts[1:]:
        gain = gain * one(*cut)
    return gain


def centred(own_key, shape, deviation, reach, split=(), held_as=jnp.bfloat16):
    drawn = jax.random.normal(own_key, shape, jnp.float32) * deviation
    if len(split) > 0:
        drawn = block_scale(own_key, shape, split, -0.22, 0.18) * drawn
    return jnp.clip(drawn, min=-reach, max=reach).astype(held_as)


def setup_inputs(seed: int = 0) -> dict:
    streams_of = jax.random.split(jax.random.key(seed), 6)
    positions = jnp.clip(1.0 * jax.random.uniform(streams_of[0], (3, NXC, NYC, NZC, SLOTS), jnp.float32) ** block_scale(streams_of[0], (3, NXC, NYC, NZC, SLOTS), ((1, 32), (3, 8)), -0.2, 0.2), 0.0, 1.0)
    cotangent = centred(streams_of[1], (3, NXC, NYC, NZC, SLOTS), 1.0, 6.0, ((1, 32), (3, 8)), jnp.float32)
    species = with_ends(jax.random.randint(streams_of[2], (NXC, NYC, NZC, SLOTS), 0, SPECIES), jax.random.fold_in(streams_of[2], 1), 0, SPECIES - 1).astype(jnp.int32)
    counts = draw_counts(jax.random.fold_in(streams_of[5], 71), 0)
    amplitude = jnp.clip(jnp.exp(jax.random.uniform(streams_of[4], (SPECIES, SPECIES), jnp.float32, math.log(0.2), math.log(2.0))), 0.2, 2.0)
    return {"positions": positions, "cotangent": cotangent, "species": species, "counts": counts, "amplitude": amplitude}


HIGHEST = lax.Precision.HIGHEST
step_size = 0.05

def pair_block(pos_home, grad_home, kind_home, live_home, pos_far, grad_far, kind_far, live_far, offset, pair_table):
    displace = pos_home[:, :, :, None] - pos_far[:, :, None, :] - offset[:, None, None, None]
    square = lax.optimization_barrier(jnp.sum(displace * displace, axis=0))
    envelope = jnp.maximum(1.0 - square, 0.0) * live_home[:, :, None] * live_far[:, None, :]
    differ = grad_home[:, :, :, None] - grad_far[:, :, None, :]
    projection = lax.optimization_barrier(jnp.sum(displace * differ, axis=0))
    mixed_row = jnp.einsum('tmb,st->smb', kind_far, pair_table, precision=HIGHEST)
    strength = jnp.einsum('sma,smb->mab', kind_home, mixed_row, precision=HIGHEST)
    response = 6.0 * strength * envelope * (envelope * differ - 4.0 * displace * projection)
    home_part = lax.optimization_barrier(jnp.sum(response, axis=3))
    away_part = -lax.optimization_barrier(jnp.sum(response, axis=2))
    weight = 6.0 * envelope * envelope * projection
    weighted = jnp.einsum('sma,mab->smb', kind_home, weight, precision=HIGHEST)
    pair_matrix = jnp.einsum('smb,tmb->st', weighted, kind_far, precision=HIGHEST)
    return (home_part, away_part, pair_matrix)

def reference(positions, cotangent, species, counts, amplitude):
    pair_table = 0.5 * (amplitude + amplitude.T)
    slots = jnp.arange(SLOTS, dtype=jnp.int32)
    live = (slots[None, None, None, :] < counts[..., None]).astype(jnp.float32)
    kinds = jnp.arange(SPECIES, dtype=jnp.int32)
    onehot = (species[None] == kinds[:, None, None, None, None]).astype(jnp.float32)
    live_field = live[None]

    def columns(field):
        return jnp.moveaxis(field, 0, 2).reshape(NXC * NYC, field.shape[0], NZC, SLOTS)
    home_cols = (columns(positions), columns(cotangent), columns(onehot), columns(live_field)[:, 0])
    total = jnp.zeros((NXC * NYC, 3, NZC, SLOTS), jnp.float32)
    matrix = jnp.zeros((SPECIES, SPECIES), jnp.float32)
    for shift_x in (-1, 0, 1):
        for shift_y in (-1, 0, 1):
            for shift_z in (-1, 0, 1):

                def rolled(field):
                    return jnp.roll(field, (-shift_x, -shift_y, -shift_z), axis=(1, 2, 3))
                far_cols = (columns(rolled(positions)), columns(rolled(cotangent)), columns(rolled(onehot)), columns(rolled(live_field))[:, 0])
                offset = jnp.array([shift_x, shift_y, shift_z], jnp.float32)

                def one_column(items):
                    home_part, away_part, pair_matrix = pair_block(*items, offset, pair_table)
                    return (home_part, pair_matrix)
                parts, mats = lax.map(one_column, home_cols + far_cols)
                total = total + parts
                matrix = matrix + lax.optimization_barrier(jnp.sum(mats, axis=0))
    total = jnp.moveaxis(total.reshape(NXC, NYC, 3, NZC, SLOTS), 2, 0)
    position_cotangent = cotangent + step_size * total
    amplitude_grad = step_size * matrix / (2.0 * math.sqrt(NCELLS / SLOTS))
    return (position_cotangent, amplitude_grad)
```

```python
import math

import jax
import jax.numpy as jnp
from jax import lax
from jax.experimental import pallas as pl
from jax.experimental.pallas import tpu as pltpu
from jax.sharding import Mesh
from jax.sharding import PartitionSpec as P

AXES = ("y_hi", "z_ax", "core", "y_lo", "x_ax")
ROW = ("y_lo", "x_ax")
COL = ("y_hi", "z_ax", "core")
NX, NZ = 32, 8
step_size = 0.05
FAR = 1.0e4
NY = 6
ZC = 4
SLOTS = 128
KINDS = 8
FEATS = 112
HOMES = NY * ZC
bf16 = jnp.bfloat16
f32 = jnp.float32


def sublane(shape=(8, SLOTS)):
    return lax.broadcasted_iota(jnp.int32, shape, 0)


def pieces(v):
    high = v.astype(bf16).astype(f32)
    rest = v - high
    mid = rest.astype(bf16).astype(f32)
    return high, mid, rest - mid


def pick(row, lo, hi, value, other):
    return jnp.where((row >= lo) & (row < hi), value, other)


def row_sum(row, lo, hi, value):
    return jnp.sum(pick(row, lo, hi, value, 0.0), axis=0, keepdims=True)


def framed(raw, row, sx, sy, sz):
    shift = jnp.where(row == 0, sx, jnp.where(row == 1, sy, jnp.where(row == 2, sz, 0.0)))
    return raw + shift.astype(f32)


def bead_terms(raw, row, shifts):
    v = framed(raw, row, *shifts)
    back = pltpu.roll(v, 3, 0)
    square = row_sum(row, 0, 3, v * v)
    cross = row_sum(row, 3, 6, v * back)
    return v, back, square, cross


def far_features(raw, shifts, lhs_ref, feat_ref, slot):
    row = sublane()
    v, back, square, cross = bead_terms(raw, row, shifts)
    code = raw[6:7]
    ahead = pltpu.roll(v, 5, 0)
    gain = jnp.where(code < 0.0, -FAR, 1.0 - square)
    a = pick(row, 0, 3, ahead, pick(row, 3, 6, back, 0.0))
    ah, am, al = pieces(a)
    qh, qm, ql = pieces(gain)
    rh, rm, rl = pieces(cross)
    one = jnp.where(row == 6, 1.0, 0.0)
    last = row == 7
    lhs = jnp.concatenate(
        [
            jnp.where(last, qh, ah + one),
            jnp.where(last, qm, ah + one),
            jnp.where(last, ql, ah + one),
            jnp.where(last, rh, am),
            jnp.where(last, rm, am),
            jnp.where(last, rl, al),
            jnp.zeros((SLOTS - 48, SLOTS), f32),
        ],
        axis=0,
    )
    lhs_ref[slot] = lhs.T.astype(bf16)
    mask = code == row.astype(f32)
    high = v.astype(bf16).astype(f32)
    low = v - high
    rows = [jnp.where(mask, 1.0, 0.0)]
    for part, start in ((high, 0), (low, 0), (high, 3), (low, 3)):
        for k in range(3):
            rows.append(jnp.where(mask, part[start + k : start + k + 1], 0.0))
    rows.append(jnp.zeros((8, SLOTS), f32))
    feat_ref[slot] = jnp.concatenate(rows, axis=0).astype(bf16)


def home_features(raw, shifts, gram_ref, frame_ref, h):
    row = sublane()
    v, back, square, cross = bead_terms(raw, row, shifts)
    square = jnp.where(raw[6:7] < 0.0, FAR, square)
    u = pick(row, 3, 6, 2.0 * back, jnp.where(row == 6, -square, 0.0))
    p = pick(row, 0, 6, -v, jnp.where(row == 6, cross, 0.0))
    last = jnp.where(row == 7, 1.0, 0.0)
    uh, um, ul = pieces(u)
    ph, pm, pl_ = pieces(p)
    gram_ref[h, :, 0:SLOTS] = jnp.concatenate(
        [uh + last, um + last, ul + last, uh, um, uh], axis=0
    ).astype(bf16)
    gram_ref[h, :, SLOTS : 2 * SLOTS] = jnp.concatenate(
        [ph, pm, pl_, ph + last, pm + last, ph + last], axis=0
    ).astype(bf16)
    frame_ref[h] = jnp.where(row == 7, cross, v)


def pair_body(steps, last, group, home_ref, far_refs, table_ref, before_ref, matrix_before_ref,
              out_ref, matrix_ref, gram_ref, frame_ref, lhs_ref, feat_ref, acc_ref,
              moment_ref, kind_ref):
    count = len(steps)
    for i, sx in enumerate(steps):
        @pl.loop(0, 48)
        def _(n, i=i, sx=sx):
            z = n // 8
            ye = n % 8
            y = lax.rem(ye + 5, 6)
            far_features(
                far_refs[i][z, y],
                (sx - 0.5, (ye - 4).astype(f32), (z - 3).astype(f32)),
                lhs_ref, feat_ref, i * 48 + n,
            )

    @pl.loop(0, HOMES)
    def _(h):
        z = h // 6
        y = h % 6
        home_features(
            home_ref[z, y], (-0.5, (y - 3).astype(f32), (z - 2).astype(f32)),
            gram_ref, frame_ref, h,
        )

    @pl.loop(0, HOMES // group)
    def _(q):
        for j in range(group):
            h = q * group + j
            z = h // 6
            y = h % 6
            gram = gram_ref[h]
            acc = None
            for i in range(count):
                base = (i * 6 + z) * 8 + y
                for dz in range(3):
                    for dy in range(3):
                        slot = base + dz * 8 + dy
                        g = jnp.dot(lhs_ref[slot, :, 0:48], gram, preferred_element_type=f32)
                        e = jnp.maximum(g[:, :SLOTS], 0.0)
                        both = jnp.concatenate([e * e, e * g[:, SLOTS:]], axis=1)
                        high = both.astype(bf16)
                        low = (both - high.astype(f32)).astype(bf16)
                        feat = feat_ref[slot]
                        part = jnp.dot(
                            jnp.concatenate([feat, feat], axis=1),
                            jnp.concatenate([high, low], axis=0),
                            preferred_element_type=f32,
                        )
                        acc = part if acc is None else acc + part
            acc_ref[h] = acc

    table = table_ref[...]

    @pl.loop(0, HOMES)
    def _(h):
        z = h // 6
        y = h % 6
        v = frame_ref[h]
        code = v[6:7]
        mix = jnp.zeros((8, SLOTS), f32)
        for s in range(KINDS):
            mix = jnp.where(code == float(s), table[:, s : s + 1], mix)

        def part(f, half):
            return acc_ref[h, 8 * f : 8 * f + 8, half * SLOTS : (half + 1) * SLOTS]

        def mixed(value):
            return jnp.sum(value * mix, axis=0, keepdims=True)

        c1 = mixed(part(0, 0))
        c2 = mixed(part(0, 1))
        moment = v[7:8] * part(0, 0)
        rows = []
        for k in range(3):
            moment = moment - v[3 + k : 4 + k] * (part(1 + k, 0) + part(4 + k, 0))
            stretch = v[3 + k : 4 + k] * c1 - mixed(part(7 + k, 0) + part(10 + k, 0))
            bend = v[k : k + 1] * c2 - mixed(part(1 + k, 1) + part(4 + k, 1))
            rows.append(step_size * (6.0 * stretch - 24.0 * bend))
        moment_ref[h] = moment
        kind_ref[h] = jnp.where(code == sublane().astype(f32), 1.0, 0.0)
        if last:
            for k in range(3):
                out_ref[k, 0, y, pl.ds(z, 1), :] = rows[k] + before_ref[z, y, k : k + 1]
        else:
            for k in range(3):
                out_ref[z, y, k : k + 1] = rows[k] + v[3 + k : 4 + k]

    total = jnp.zeros((8, 8), f32)
    moments = jnp.concatenate([moment_ref[h] for h in range(HOMES)], axis=1)
    kinds = jnp.concatenate([kind_ref[h] for h in range(HOMES)], axis=1).astype(bf16)
    for piece in pieces(moments):
        total = total + lax.dot_general(
            piece.astype(bf16), kinds, (((1,), (1,)), ((), ())), preferred_element_type=f32
        )
    if last:
        total = total + matrix_before_ref[...]
    matrix_ref[...] = total


def pair_call(steps, last, group, home, fars, table, before, matrix_before):
    count = len(steps)
    vmem = pl.BlockSpec(memory_space=pltpu.VMEM)

    def body(home_ref, *refs):
        far_refs = refs[:count]
        table_ref = refs[count]
        rest = refs[count + 1 :]
        if last:
            before_ref, matrix_before_ref = rest[:2]
            rest = rest[2:]
        else:
            before_ref = matrix_before_ref = None
        pair_body(steps, last, group, home_ref, far_refs, table_ref, before_ref,
                  matrix_before_ref, *rest)

    out = (
        jax.ShapeDtypeStruct((3, 1, NY, ZC, SLOTS), f32)
        if last
        else jax.ShapeDtypeStruct((ZC, NY, 8, SLOTS), f32)
    )
    operands = [home, *fars, table]
    if last:
        operands += [before, matrix_before]
    return pl.pallas_call(
        body,
        out_shape=(out, jax.ShapeDtypeStruct((8, 8), f32)),
        in_specs=[vmem] * len(operands),
        out_specs=(vmem, vmem),
        scratch_shapes=[
            pltpu.VMEM((HOMES, 48, 2 * SLOTS), bf16),
            pltpu.VMEM((HOMES, 8, SLOTS), f32),
            pltpu.VMEM((48 * count, SLOTS, SLOTS), bf16),
            pltpu.VMEM((48 * count, FEATS, SLOTS), bf16),
            pltpu.VMEM((HOMES, FEATS, 2 * SLOTS), f32),
            pltpu.VMEM((HOMES, 8, SLOTS), f32),
            pltpu.VMEM((HOMES, 8, SLOTS), f32),
        ],
        compiler_params=pltpu.CompilerParams(vmem_limit_bytes=48 * 2**20),
        name="pairs_last" if last else "pairs_first",
    )(*operands)


def pack_body(counts_ref, pos_ref, cot_ref, species_ref, out_ref, low_ref, high_ref):
    lane = lax.broadcasted_iota(jnp.int32, (1, SLOTS), 1)
    for y in range(NY):
        for z in range(ZC):
            rows = [pos_ref[k, 0, y, z : z + 1, :] for k in range(3)]
            rows += [cot_ref[k, 0, y, z : z + 1, :] for k in range(3)]
            kind = jnp.where(lane < counts_ref[0, y, z], species_ref[0, y, z : z + 1, :], -1)
            rows += [kind.astype(f32), jnp.zeros((1, SLOTS), f32)]
            packed = jnp.concatenate(rows, axis=0)
            out_ref[z, y] = packed
            if z == 0:
                low_ref[0, y] = packed
            if z == ZC - 1:
                high_ref[0, y] = packed


def pack(counts, positions, cotangent, species):
    vmem = pl.BlockSpec(memory_space=pltpu.VMEM)
    return pl.pallas_call(
        pack_body,
        out_shape=(
            jax.ShapeDtypeStruct((ZC, NY, 8, SLOTS), f32),
            jax.ShapeDtypeStruct((1, NY, 8, SLOTS), f32),
            jax.ShapeDtypeStruct((1, NY, 8, SLOTS), f32),
        ),
        in_specs=[pl.BlockSpec(memory_space=pltpu.SMEM)] + [vmem] * 3,
        out_specs=(vmem,) * 3,
        name="pack",
    )(counts, positions, cotangent, species)


def move(block, dx, dz):
    pairs = []
    for i in range(NX):
        for j in range(NZ):
            pairs.append((i * NZ + j, (i + dx) % NX * NZ + (j + dz) % NZ))
    return lax.ppermute(block, AXES, pairs)


def summed(matrix):
    for group in (("core", "y_lo", "x_ax"), ("y_hi", "z_ax")):
        n = lax.axis_size(group)
        sent = jnp.broadcast_to(matrix[None], (n,) + matrix.shape)
        matrix = jnp.sum(lax.all_to_all(sent, group, 0, 0), axis=0)
    return matrix


def per_device(positions, cotangent, species, counts, amplitude):
    table = 0.5 * (amplitude + amplitude.T)
    home, low, high = pack(counts, positions, cotangent, species)
    below = move(high, 0, 1)
    above = move(low, 0, -1)
    column = jnp.concatenate([below, home, above], axis=0)
    left = move(column, 1, 0)
    right = move(column, -1, 0)
    part, matrix_part = pair_call((0.0,), False, 3, home, (column,), table, None, None)
    out, matrix = pair_call(
        (-1.0, 1.0), True, 2, home, (left, right), table, part, matrix_part
    )
    cells_total = NX * NY * NZ * ZC
    total = 6.0 * summed(matrix + matrix.T)
    return out, step_size * total / (2.0 * math.sqrt(cells_total / SLOTS))


def solution(mesh):
    finer = Mesh(mesh.devices.reshape(2, 8, 2, 2, 4), AXES)
    in_specs = (
        P(None, COL, None, ROW, None),
        P(None, COL, None, ROW, None),
        P(COL, None, ROW, None),
        P(COL, None, ROW),
        P(),
    )
    return jax.shard_map(
        per_device,
        mesh=finer,
        in_specs=in_specs,
        out_specs=(P(None, COL, None, ROW, None), P()),
        check_vma=False,
    )
```

```python
import math

import jax
import jax.numpy as jnp
from jax import lax
from jax.experimental import pallas as pl
from jax.experimental.pallas import tpu as pltpu
from jax.sharding import Mesh
from jax.sharding import PartitionSpec as P

AXES = ("y_hi", "z_ax", "core", "y_lo", "x_ax")
ROW = ("y_lo", "x_ax")
COL = ("y_hi", "z_ax", "core")
NX, NZ = 32, 8
step_size = 0.05
FAR = 1.0e4
NY = 6
ZC = 4
SLOTS = 128
KINDS = 8
FEATS = 112
HOMES = NY * ZC
bf16 = jnp.bfloat16
f32 = jnp.float32


def sublane(shape=(8, SLOTS)):
    return lax.broadcasted_iota(jnp.int32, shape, 0)


def pieces(v):
    high = v.astype(bf16).astype(f32)
    rest = v - high
    mid = rest.astype(bf16).astype(f32)
    return high, mid, rest - mid


def pick(row, lo, hi, value, other):
    return jnp.where((row >= lo) & (row < hi), value, other)


def row_sum(row, lo, hi, value):
    return jnp.sum(pick(row, lo, hi, value, 0.0), axis=0, keepdims=True)


def framed(raw, row, sx, sy, sz):
    shift = jnp.where(row == 0, sx, jnp.where(row == 1, sy, jnp.where(row == 2, sz, 0.0)))
    return raw + shift.astype(f32)


def bead_terms(raw, row, shifts):
    v = framed(raw, row, *shifts)
    back = pltpu.roll(v, 3, 0)
    square = row_sum(row, 0, 3, v * v)
    cross = row_sum(row, 3, 6, v * back)
    return v, back, square, cross


def far_features(raw, shifts, lhs_ref, feat_ref, slot):
    row = sublane()
    v, back, square, cross = bead_terms(raw, row, shifts)
    code = raw[6:7]
    ahead = pltpu.roll(v, 5, 0)
    gain = jnp.where(code < 0.0, -FAR, 1.0 - square)
    a = pick(row, 0, 3, ahead, pick(row, 3, 6, back, 0.0))
    ah, am, al = pieces(a)
    qh, qm, ql = pieces(gain)
    rh, rm, rl = pieces(cross)
    one = jnp.where(row == 6, 1.0, 0.0)
    last = row == 7
    lhs = jnp.concatenate(
        [
            jnp.where(last, qh, ah + one),
            jnp.where(last, qm, ah + one),
            jnp.where(last, ql, ah + one),
            jnp.where(last, rh, am),
            jnp.where(last, rm, am),
            jnp.where(last, rl, al),
            jnp.zeros((SLOTS - 48, SLOTS), f32),
        ],
        axis=0,
    )
    lhs_ref[slot] = lhs.T.astype(bf16)
    mask = code == row.astype(f32)
    high = v.astype(bf16).astype(f32)
    low = v - high
    rows = [jnp.where(mask, 1.0, 0.0)]
    for part, start in ((high, 0), (low, 0), (high, 3), (low, 3)):
        for k in range(3):
            rows.append(jnp.where(mask, part[start + k : start + k + 1], 0.0))
    rows.append(jnp.zeros((8, SLOTS), f32))
    feat_ref[slot] = jnp.concatenate(rows, axis=0).astype(bf16)


def home_features(raw, shifts, gram_ref, frame_ref, h):
    row = sublane()
    v, back, square, cross = bead_terms(raw, row, shifts)
    square = jnp.where(raw[6:7] < 0.0, FAR, square)
    u = pick(row, 3, 6, 2.0 * back, jnp.where(row == 6, -square, 0.0))
    p = pick(row, 0, 6, -v, jnp.where(row == 6, cross, 0.0))
    last = jnp.where(row == 7, 1.0, 0.0)
    uh, um, ul = pieces(u)
    ph, pm, pl_ = pieces(p)
    gram_ref[h, :, 0:SLOTS] = jnp.concatenate(
        [uh + last, um + last, ul + last, uh, um, uh], axis=0
    ).astype(bf16)
    gram_ref[h, :, SLOTS : 2 * SLOTS] = jnp.concatenate(
        [ph, pm, pl_, ph + last, pm + last, ph + last], axis=0
    ).astype(bf16)
    frame_ref[h] = jnp.where(row == 7, cross, v)


def pair_body(steps, last, group, home_ref, far_refs, table_ref, before_ref, matrix_before_ref,
              out_ref, matrix_ref, gram_ref, frame_ref, lhs_ref, feat_ref, acc_ref,
              moment_ref, kind_ref):
    count = len(steps)
    for i, sx in enumerate(steps):
        @pl.loop(0, 48, unroll=4)
        def _(n, i=i, sx=sx):
            z = n // 8
            ye = n % 8
            y = lax.rem(ye + 5, 6)
            far_features(
                far_refs[i][z, y],
                (sx - 0.5, (ye - 4).astype(f32), (z - 3).astype(f32)),
                lhs_ref, feat_ref, i * 48 + n,
            )

    @pl.loop(0, HOMES, unroll=4)
    def _(h):
        z = h // 6
        y = h % 6
        home_features(
            home_ref[z, y], (-0.5, (y - 3).astype(f32), (z - 2).astype(f32)),
            gram_ref, frame_ref, h,
        )

    @pl.loop(0, HOMES // group)
    def _(q):
        for j in range(group):
            h = q * group + j
            z = h // 6
            y = h % 6
            gram = gram_ref[h]
            acc = None
            for i in range(count):
                base = (i * 6 + z) * 8 + y
                for dz in range(3):
                    for dy in range(3):
                        slot = base + dz * 8 + dy
                        g = jnp.dot(lhs_ref[slot, :, 0:48], gram, preferred_element_type=f32)
                        e = jnp.maximum(g[:, :SLOTS], 0.0)
                        both = jnp.concatenate([e * e, e * g[:, SLOTS:]], axis=1)
                        high = both.astype(bf16)
                        low = (both - high.astype(f32)).astype(bf16)
                        feat = feat_ref[slot]
                        part = jnp.dot(
                            jnp.concatenate([feat, feat], axis=1),
                            jnp.concatenate([high, low], axis=0),
                            preferred_element_type=f32,
                        )
                        acc = part if acc is None else acc + part
            acc_ref[h] = acc

    table = table_ref[...]
    columns = [jnp.broadcast_to(table[:, s : s + 1], (8, SLOTS)) for s in range(KINDS)]

    @pl.loop(0, HOMES, unroll=4)
    def _(h):
        z = h // 6
        y = h % 6
        v = frame_ref[h]
        code = v[6:7]
        mix = jnp.zeros((8, SLOTS), f32)
        for s in range(KINDS):
            mix = jnp.where(code == float(s), columns[s], mix)

        def part(f, half):
            return acc_ref[h, 8 * f : 8 * f + 8, half * SLOTS : (half + 1) * SLOTS]

        def mixed(value):
            return jnp.sum(value * mix, axis=0, keepdims=True)

        c1 = mixed(part(0, 0))
        c2 = mixed(part(0, 1))
        moment = v[7:8] * part(0, 0)
        rows = []
        for k in range(3):
            moment = moment - v[3 + k : 4 + k] * (part(1 + k, 0) + part(4 + k, 0))
            stretch = v[3 + k : 4 + k] * c1 - mixed(part(7 + k, 0) + part(10 + k, 0))
            bend = v[k : k + 1] * c2 - mixed(part(1 + k, 1) + part(4 + k, 1))
            rows.append(step_size * (6.0 * stretch - 24.0 * bend))
        moment_ref[h] = moment
        kind_ref[h] = jnp.where(code == sublane().astype(f32), 1.0, 0.0)
        if last:
            for k in range(3):
                out_ref[k, 0, y, pl.ds(z, 1), :] = rows[k] + before_ref[z, y, k : k + 1]
        else:
            for k in range(3):
                out_ref[z, y, k : k + 1] = rows[k] + v[3 + k : 4 + k]

    total = jnp.zeros((8, 8), f32)
    moments = jnp.concatenate([moment_ref[h] for h in range(HOMES)], axis=1)
    kinds = jnp.concatenate([kind_ref[h] for h in range(HOMES)], axis=1).astype(bf16)
    for piece in pieces(moments):
        total = total + lax.dot_general(
            piece.astype(bf16), kinds, (((1,), (1,)), ((), ())), preferred_element_type=f32
        )
    if last:
        total = total + matrix_before_ref[...]
    matrix_ref[...] = total


def pair_call(steps, last, group, home, fars, table, before, matrix_before):
    count = len(steps)
    vmem = pl.BlockSpec(memory_space=pltpu.VMEM)

    def body(home_ref, *refs):
        far_refs = refs[:count]
        table_ref = refs[count]
        rest = refs[count + 1 :]
        if last:
            before_ref, matrix_before_ref = rest[:2]
            rest = rest[2:]
        else:
            before_ref = matrix_before_ref = None
        pair_body(steps, last, group, home_ref, far_refs, table_ref, before_ref,
                  matrix_before_ref, *rest)

    out = (
        jax.ShapeDtypeStruct((3, 1, NY, ZC, SLOTS), f32)
        if last
        else jax.ShapeDtypeStruct((ZC, NY, 8, SLOTS), f32)
    )
    operands = [home, *fars, table]
    if last:
        operands += [before, matrix_before]
    return pl.pallas_call(
        body,
        out_shape=(out, jax.ShapeDtypeStruct((8, 8), f32)),
        in_specs=[vmem] * len(operands),
        out_specs=(vmem, vmem),
        scratch_shapes=[
            pltpu.VMEM((HOMES, 48, 2 * SLOTS), bf16),
            pltpu.VMEM((HOMES, 8, SLOTS), f32),
            pltpu.VMEM((48 * count, SLOTS, SLOTS), bf16),
            pltpu.VMEM((48 * count, FEATS, SLOTS), bf16),
            pltpu.VMEM((HOMES, FEATS, 2 * SLOTS), f32),
            pltpu.VMEM((HOMES, 8, SLOTS), f32),
            pltpu.VMEM((HOMES, 8, SLOTS), f32),
        ],
        compiler_params=pltpu.CompilerParams(vmem_limit_bytes=48 * 2**20),
        name="pairs_last" if last else "pairs_first",
    )(*operands)


def pack_body(counts_ref, pos_ref, cot_ref, species_ref, out_ref, low_ref, high_ref):
    lane = lax.broadcasted_iota(jnp.int32, (1, SLOTS), 1)
    for y in range(NY):
        for z in range(ZC):
            rows = [pos_ref[k, 0, y, z : z + 1, :] for k in range(3)]
            rows += [cot_ref[k, 0, y, z : z + 1, :] for k in range(3)]
            kind = jnp.where(lane < counts_ref[0, y, z], species_ref[0, y, z : z + 1, :], -1)
            rows += [kind.astype(f32), jnp.zeros((1, SLOTS), f32)]
            packed = jnp.concatenate(rows, axis=0)
            out_ref[z, y] = packed
            if z == 0:
                low_ref[0, y] = packed
            if z == ZC - 1:
                high_ref[0, y] = packed


def pack(counts, positions, cotangent, species):
    vmem = pl.BlockSpec(memory_space=pltpu.VMEM)
    return pl.pallas_call(
        pack_body,
        out_shape=(
            jax.ShapeDtypeStruct((ZC, NY, 8, SLOTS), f32),
            jax.ShapeDtypeStruct((1, NY, 8, SLOTS), f32),
            jax.ShapeDtypeStruct((1, NY, 8, SLOTS), f32),
        ),
        in_specs=[pl.BlockSpec(memory_space=pltpu.SMEM)] + [vmem] * 3,
        out_specs=(vmem,) * 3,
        name="pack",
    )(counts, positions, cotangent, species)


def move(block, dx, dz):
    pairs = []
    for i in range(NX):
        for j in range(NZ):
            pairs.append((i * NZ + j, (i + dx) % NX * NZ + (j + dz) % NZ))
    return lax.ppermute(block, AXES, pairs)


def summed(matrix):
    sent = jnp.broadcast_to(matrix.reshape(1, KINDS * KINDS), (NX * NZ, KINDS * KINDS))
    heard = lax.all_to_all(sent, AXES, 0, 0, tiled=True)
    return jnp.sum(heard, axis=0).reshape(KINDS, KINDS)


def per_device(positions, cotangent, species, counts, amplitude):
    table = 0.5 * (amplitude + amplitude.T)
    home, low, high = pack(counts, positions, cotangent, species)
    below = move(high, 0, 1)
    above = move(low, 0, -1)
    column = jnp.concatenate([below, home, above], axis=0)
    left = move(column, 1, 0)
    right = move(column, -1, 0)
    part, matrix_part = pair_call((0.0,), False, 3, home, (column,), table, None, None)
    out, matrix = pair_call(
        (-1.0, 1.0), True, 2, home, (left, right), table, part, matrix_part
    )
    cells_total = NX * NY * NZ * ZC
    total = 6.0 * summed(matrix + matrix.T)
    return out, step_size * total / (2.0 * math.sqrt(cells_total / SLOTS))


def solution(mesh):
    finer = Mesh(mesh.devices.reshape(2, 8, 2, 2, 4), AXES)
    in_specs = (
        P(None, COL, None, ROW, None),
        P(None, COL, None, ROW, None),
        P(COL, None, ROW, None),
        P(COL, None, ROW),
        P(),
    )
    return jax.shard_map(
        per_device,
        mesh=finer,
        in_specs=in_specs,
        out_specs=(P(None, COL, None, ROW, None), P()),
        check_vma=False,
    )
```

```python
import math

import jax
import jax.numpy as jnp
from jax import lax
from jax.experimental import pallas as pl
from jax.experimental.pallas import tpu as pltpu
from jax.sharding import Mesh
from jax.sharding import PartitionSpec as P

AXES = ("y_hi", "z_ax", "core", "y_lo", "x_ax")
ROW = ("y_lo", "x_ax")
COL = ("y_hi", "z_ax", "core")
NX, NZ = 32, 8
step_size = 0.05
FAR = 1.0e4
NY = 6
ZC = 4
SLOTS = 128
KINDS = 8
HOMES = NY * ZC
bf16 = jnp.bfloat16
f32 = jnp.float32


def sublane(shape=(8, SLOTS)):
    return lax.broadcasted_iota(jnp.int32, shape, 0)


def pieces(v):
    high = v.astype(bf16).astype(f32)
    rest = v - high
    mid = rest.astype(bf16).astype(f32)
    return high, mid, rest - mid


def pick(row, lo, hi, value, other):
    return jnp.where((row >= lo) & (row < hi), value, other)


def row_sum(row, lo, hi, value):
    return jnp.sum(pick(row, lo, hi, value, 0.0), axis=0, keepdims=True)


def framed(raw, row, sx, sy, sz):
    shift = jnp.where(row == 0, sx, jnp.where(row == 1, sy, jnp.where(row == 2, sz, 0.0)))
    return raw + shift.astype(f32)


def bead_terms(raw, row, shifts):
    v = framed(raw, row, *shifts)
    back = pltpu.roll(v, 3, 0)
    square = row_sum(row, 0, 3, v * v)
    cross = row_sum(row, 3, 6, v * back)
    return v, back, square, cross


def far_features(raw, shifts, lhs_ref, feat_ref, slot):
    row = sublane()
    v, back, square, cross = bead_terms(raw, row, shifts)
    code = raw[6:7]
    ahead = pltpu.roll(v, 5, 0)
    gain = jnp.where(code < 0.0, -FAR, 1.0 - square)
    a = pick(row, 0, 3, ahead, pick(row, 3, 6, back, 0.0))
    ah, am, al = pieces(a)
    qh, qm, ql = pieces(gain)
    rh, rm, rl = pieces(cross)
    one = jnp.where(row == 6, 1.0, 0.0)
    last = row == 7
    lhs = jnp.concatenate(
        [
            jnp.where(last, qh, ah + one),
            jnp.where(last, qm, ah + one),
            jnp.where(last, ql, ah + one),
            jnp.where(last, rh, am),
            jnp.where(last, rm, am),
            jnp.where(last, rl, al),
            jnp.zeros((SLOTS - 48, SLOTS), f32),
        ],
        axis=0,
    )
    lhs_ref[slot] = lhs.T.astype(bf16)
    mask = code == row.astype(f32)
    high = v.astype(bf16).astype(f32)
    low = v - high
    rows = [jnp.where(mask, 1.0, 0.0)]
    for part, start in ((high, 0), (low, 0), (high, 3), (low, 3)):
        for k in range(3):
            rows.append(jnp.where(mask, part[start + k : start + k + 1], 0.0))
    if feat_ref.shape[1] == 128:
        rows += [jnp.where(mask, r, 0.0) for r in (rh, rm, rl)]
    else:
        rows.append(jnp.zeros((8, SLOTS), f32))
    feat_ref[slot] = jnp.concatenate(rows, axis=0).astype(bf16)


def home_features(raw, shifts, gram_ref, frame_ref, h):
    row = sublane()
    v, back, square, cross = bead_terms(raw, row, shifts)
    square = jnp.where(raw[6:7] < 0.0, FAR, square)
    u = pick(row, 3, 6, 2.0 * back, jnp.where(row == 6, -square, 0.0))
    p = pick(row, 0, 6, -v, jnp.where(row == 6, cross, 0.0))
    last = jnp.where(row == 7, 1.0, 0.0)
    uh, um, ul = pieces(u)
    ph, pm, pl_ = pieces(p)
    gram_ref[h, :, 0:SLOTS] = jnp.concatenate(
        [uh + last, um + last, ul + last, uh, um, uh], axis=0
    ).astype(bf16)
    gram_ref[h, :, SLOTS : 2 * SLOTS] = jnp.concatenate(
        [ph, pm, pl_, ph + last, pm + last, ph + last], axis=0
    ).astype(bf16)
    frame_ref[h] = jnp.where(row == 7, cross, v)


def pair_body(steps, tiles, group, stage, home_ref, far_refs, table_ref, before_ref,
              matrix_before_ref, out_ref, matrix_ref, gram_ref, frame_ref, lhs_ref, feat_ref,
              acc_ref, own_ref, moment_ref, kind_ref):
    for i, sx in enumerate(steps):
        @pl.loop(0, 48, unroll=4)
        def _(n, i=i, sx=sx):
            z = n // 8
            ye = n % 8
            y = lax.rem(ye + 5, 6)
            far_features(
                far_refs[i][z, y],
                (sx - 0.5, (ye - 4).astype(f32), (z - 3).astype(f32)),
                lhs_ref, feat_ref, i * 48 + n,
            )

    @pl.loop(0, HOMES, unroll=4)
    def _(h):
        z = h // 6
        y = h % 6
        home_features(
            home_ref[z, y], (-0.5, (y - 3).astype(f32), (z - 2).astype(f32)),
            gram_ref, frame_ref, h,
        )

    @pl.loop(0, HOMES // group)
    def _(q):
        for j in range(group):
            h = q * group + j
            z = h // 6
            y = h % 6
            gram = gram_ref[h]
            acc = None
            for i, dz, dy in tiles:
                slot = (i * 6 + z + dz) * 8 + y + dy
                g = jnp.dot(lhs_ref[slot, :, 0:48], gram, preferred_element_type=f32)
                e = jnp.maximum(g[:, :SLOTS], 0.0)
                both = jnp.concatenate([e * e, e * g[:, SLOTS:]], axis=1)
                high = both.astype(bf16)
                low = (both - high.astype(f32)).astype(bf16)
                feat = feat_ref[slot]
                part = jnp.dot(
                    jnp.concatenate([feat, feat], axis=1),
                    jnp.concatenate([high, low], axis=0),
                    preferred_element_type=f32,
                )
                if stage == 0 and acc is None:
                    own_ref[h] = part[56:, :SLOTS]
                acc = part if acc is None else acc + part
            acc_ref[h] = acc

    table = table_ref[...]
    columns = [jnp.broadcast_to(table[:, s : s + 1], (8, SLOTS)) for s in range(KINDS)]

    @pl.loop(0, HOMES, unroll=4)
    def _(h):
        z = h // 6
        y = h % 6
        v = frame_ref[h]
        code = v[6:7]
        mix = jnp.zeros((8, SLOTS), f32)
        for s in range(KINDS):
            mix = jnp.where(code == float(s), columns[s], mix)

        def part(f, half):
            return acc_ref[h, 8 * f : 8 * f + 8, half * SLOTS : (half + 1) * SLOTS]

        def mixed(value):
            return jnp.sum(value * mix, axis=0, keepdims=True)

        def away(f):
            if stage == 0:
                return part(f, 0) - own_ref[h, 8 * f - 56 : 8 * f - 48]
            return part(f, 0)

        c1 = mixed(part(0, 0))
        c2 = mixed(part(0, 1))
        rows = []
        for k in range(3):
            stretch = v[3 + k : 4 + k] * c1 - mixed(part(7 + k, 0) + part(10 + k, 0))
            bend = v[k : k + 1] * c2 - mixed(part(1 + k, 1) + part(4 + k, 1))
            rows.append(step_size * (6.0 * stretch - 24.0 * bend))
        if stage < 2:
            moment = v[7:8] * part(0, 0) + (away(13) + away(14) + away(15))
            for k in range(3):
                moment = moment - v[3 + k : 4 + k] * (part(1 + k, 0) + part(4 + k, 0))
                moment = moment - v[k : k + 1] * (away(7 + k) + away(10 + k))
            moment_ref[h] = moment
            kind_ref[h] = jnp.where(code == sublane().astype(f32), 1.0, 0.0)
        for k in range(3):
            if stage == 2:
                out_ref[k, 0, y, pl.ds(z, 1), :] = rows[k] + before_ref[z, y, k : k + 1]
            else:
                old = v[3 + k : 4 + k] if stage == 0 else before_ref[z, y, k : k + 1]
                out_ref[z, y, k : k + 1] = rows[k] + old

    if stage < 2:
        total = jnp.zeros((8, 8), f32)
        moments = jnp.concatenate([moment_ref[h] for h in range(HOMES)], axis=1)
        kinds = jnp.concatenate([kind_ref[h] for h in range(HOMES)], axis=1).astype(bf16)
        for piece in pieces(moments):
            total = total + lax.dot_general(
                piece.astype(bf16), kinds, (((1,), (1,)), ((), ())), preferred_element_type=f32
            )
        if stage == 1:
            total = total + matrix_before_ref[...]
        matrix_ref[...] = total


def pair_call(steps, tiles, group, stage, home, fars, table, before=None, matrix_before=None):
    count = len(steps)
    feats = 112 if stage == 2 else 128
    vmem = pl.BlockSpec(memory_space=pltpu.VMEM)
    operands = [home, *fars, table]
    if stage > 0:
        operands.append(before)
    if stage == 1:
        operands.append(matrix_before)
    scratch = [
        pltpu.VMEM((HOMES, 48, 2 * SLOTS), bf16),
        pltpu.VMEM((HOMES, 8, SLOTS), f32),
        pltpu.VMEM((48 * count, SLOTS, SLOTS), bf16),
        pltpu.VMEM((48 * count, feats, SLOTS), bf16),
        pltpu.VMEM((HOMES, feats, 2 * SLOTS), f32),
    ]
    if stage < 2:
        scratch += [pltpu.VMEM((HOMES, 72, SLOTS), f32)] + [pltpu.VMEM((HOMES, 8, SLOTS), f32)] * 2

    def body(home_ref, *refs):
        far_refs = refs[:count]
        table_ref = refs[count]
        refs = list(refs[count + 1 :])
        before_ref = refs.pop(0) if stage > 0 else None
        matrix_before_ref = refs.pop(0) if stage == 1 else None
        out_ref = refs.pop(0)
        matrix_ref = refs.pop(0) if stage < 2 else None
        if stage == 2:
            refs += [None] * 3
        pair_body(steps, tiles, group, stage, home_ref, far_refs, table_ref, before_ref,
                  matrix_before_ref, out_ref, matrix_ref, *refs)

    if stage == 2:
        out = (jax.ShapeDtypeStruct((3, 1, NY, ZC, SLOTS), f32),)
    else:
        out = (
            jax.ShapeDtypeStruct((ZC, NY, 8, SLOTS), f32),
            jax.ShapeDtypeStruct((8, 8), f32),
        )
    return pl.pallas_call(
        body,
        out_shape=out,
        in_specs=[vmem] * len(operands),
        out_specs=(vmem,) * len(out),
        scratch_shapes=scratch,
        compiler_params=pltpu.CompilerParams(vmem_limit_bytes=48 * 2**20),
        name=("pairs_own", "pairs_left", "pairs_rest")[stage],
    )(*operands)


def pack_body(counts_ref, pos_ref, cot_ref, species_ref, out_ref, low_ref, high_ref):
    lane = lax.broadcasted_iota(jnp.int32, (1, SLOTS), 1)
    for y in range(NY):
        for z in range(ZC):
            rows = [pos_ref[k, 0, y, z : z + 1, :] for k in range(3)]
            rows += [cot_ref[k, 0, y, z : z + 1, :] for k in range(3)]
            kind = jnp.where(lane < counts_ref[0, y, z], species_ref[0, y, z : z + 1, :], -1)
            rows += [kind.astype(f32), jnp.zeros((1, SLOTS), f32)]
            packed = jnp.concatenate(rows, axis=0)
            out_ref[z, y] = packed
            if z == 0:
                low_ref[0, y] = packed
            if z == ZC - 1:
                high_ref[0, y] = packed


def pack(counts, positions, cotangent, species):
    vmem = pl.BlockSpec(memory_space=pltpu.VMEM)
    return pl.pallas_call(
        pack_body,
        out_shape=(
            jax.ShapeDtypeStruct((ZC, NY, 8, SLOTS), f32),
            jax.ShapeDtypeStruct((1, NY, 8, SLOTS), f32),
            jax.ShapeDtypeStruct((1, NY, 8, SLOTS), f32),
        ),
        in_specs=[pl.BlockSpec(memory_space=pltpu.SMEM)] + [vmem] * 3,
        out_specs=(vmem,) * 3,
        name="pack",
    )(counts, positions, cotangent, species)


def move(block, dx, dz):
    pairs = []
    for i in range(NX):
        for j in range(NZ):
            pairs.append((i * NZ + j, (i + dx) % NX * NZ + (j + dz) % NZ))
    return lax.ppermute(block, AXES, pairs)


OWN_HALF = [(0, 1, 1), (0, 1, 2), (0, 2, 0), (0, 2, 1), (0, 2, 2)]
OWN_OTHER = [(0, 1, 0), (0, 0, 0), (0, 0, 1), (0, 0, 2)]


def whole(i):
    return [(i, dz, dy) for dz in range(3) for dy in range(3)]


def per_device(positions, cotangent, species, counts, amplitude):
    table = 0.5 * (amplitude + amplitude.T)
    home, low, high = pack(counts, positions, cotangent, species)
    below = move(high, 0, 1)
    above = move(low, 0, -1)
    column = jnp.concatenate([below, home, above], axis=0)
    left = move(column, 1, 0)
    right = move(column, -1, 0)
    part, matrix = pair_call((0.0,), OWN_HALF, 4, 0, home, (column,), table)
    part, matrix = pair_call((-1.0,), whole(0), 3, 1, home, (left,), table, part, matrix)
    sent = jnp.broadcast_to(matrix.reshape(1, KINDS * KINDS), (NX * NZ, KINDS * KINDS))
    sent, part = lax.optimization_barrier((sent, part))
    heard = lax.all_to_all(sent, AXES, 0, 0, tiled=True)
    (out,) = pair_call(
        (0.0, 1.0), OWN_OTHER + whole(1), 2, 2, home, (column, right), table, part
    )
    heard, out = lax.optimization_barrier((heard, out))
    matrix = jnp.sum(heard, axis=0).reshape(KINDS, KINDS)
    cells_total = NX * NY * NZ * ZC
    total = 6.0 * (matrix + matrix.T)
    return out, step_size * total / (2.0 * math.sqrt(cells_total / SLOTS))


def solution(mesh):
    finer = Mesh(mesh.devices.reshape(2, 8, 2, 2, 4), AXES)
    in_specs = (
        P(None, COL, None, ROW, None),
        P(None, COL, None, ROW, None),
        P(COL, None, ROW, None),
        P(COL, None, ROW),
        P(),
    )
    return jax.shard_map(
        per_device,
        mesh=finer,
        in_specs=in_specs,
        out_specs=(P(None, COL, None, ROW, None), P()),
        check_vma=False,
    )
```

```python
import math

import jax
import jax.numpy as jnp
from jax import lax
from jax.experimental import pallas as pl
from jax.experimental.pallas import tpu as pltpu
from jax.sharding import Mesh
from jax.sharding import PartitionSpec as P

AXES = ("y_hi", "z_ax", "core", "y_lo", "x_ax")
ROW = ("y_lo", "x_ax")
COL = ("y_hi", "z_ax", "core")
NX, NZ = 32, 8
step_size = 0.05
FAR = 1.0e4
NY = 6
ZC = 4
SLOTS = 128
KINDS = 8
SHORT = 32
HOMES = NY * ZC
bf16 = jnp.bfloat16
f32 = jnp.float32


def sublane(shape=(8, SLOTS)):
    return lax.broadcasted_iota(jnp.int32, shape, 0)


def pieces(v):
    high = v.astype(bf16).astype(f32)
    rest = v - high
    mid = rest.astype(bf16).astype(f32)
    return high, mid, rest - mid


def pick(row, lo, hi, value, other):
    return jnp.where((row >= lo) & (row < hi), value, other)


def row_sum(row, lo, hi, value):
    return jnp.sum(pick(row, lo, hi, value, 0.0), axis=0, keepdims=True)


def framed(raw, row, sx, sy, sz):
    shift = jnp.where(row == 0, sx, jnp.where(row == 1, sy, jnp.where(row == 2, sz, 0.0)))
    return raw + shift.astype(f32)


def bead_terms(v, row):
    back = pltpu.roll(v, 3, 0)
    square = row_sum(row, 0, 3, v * v)
    cross = row_sum(row, 3, 6, v * back)
    return back, square, cross


def far_features(v, lhs_ref, feat_ref, slot):
    row = sublane()
    back, square, cross = bead_terms(v, row)
    code = v[6:7]
    ahead = pltpu.roll(v, 5, 0)
    gain = jnp.where(code < 0.0, -FAR, 1.0 - square)
    a = pick(row, 0, 3, ahead, pick(row, 3, 6, back, 0.0))
    ah, am, al = pieces(a)
    qh, qm, ql = pieces(gain)
    rh, rm, rl = pieces(cross)
    one = jnp.where(row == 6, 1.0, 0.0)
    last = row == 7
    lhs = jnp.concatenate(
        [
            jnp.where(last, qh, ah + one),
            jnp.where(last, qm, ah + one),
            jnp.where(last, ql, ah + one),
            jnp.where(last, rh, am),
            jnp.where(last, rm, am),
            jnp.where(last, rl, al),
            jnp.zeros((SLOTS - 48, SLOTS), f32),
        ],
        axis=0,
    )
    lhs_ref[slot] = lhs.T.astype(bf16)
    mask = code == row.astype(f32)
    high = v.astype(bf16).astype(f32)
    low = v - high
    rows = [jnp.where(mask, 1.0, 0.0)]
    for part, start in ((high, 0), (low, 0), (high, 3), (low, 3)):
        for k in range(3):
            rows.append(jnp.where(mask, part[start + k : start + k + 1], 0.0))
    if feat_ref.shape[1] == 128:
        rows += [jnp.where(mask, r, 0.0) for r in (rh, rm, rl)]
    else:
        rows.append(jnp.zeros((8, SLOTS), f32))
    feat_ref[slot] = jnp.concatenate(rows, axis=0).astype(bf16)


def home_features(v, gram_ref, frame_ref, h):
    row = sublane()
    back, square, cross = bead_terms(v, row)
    square = jnp.where(v[6:7] < 0.0, FAR, square)
    u = pick(row, 3, 6, 2.0 * back, jnp.where(row == 6, -square, 0.0))
    p = pick(row, 0, 6, -v, jnp.where(row == 6, cross, 0.0))
    last = jnp.where(row == 7, 1.0, 0.0)
    uh, um, ul = pieces(u)
    ph, pm, pl_ = pieces(p)
    gram_ref[h, :, 0:SLOTS] = jnp.concatenate(
        [uh + last, um + last, ul + last, uh, um, uh], axis=0
    ).astype(bf16)
    gram_ref[h, :, SLOTS : 2 * SLOTS] = jnp.concatenate(
        [ph, pm, pl_, ph + last, pm + last, ph + last], axis=0
    ).astype(bf16)
    frame_ref[h] = jnp.where(row == 7, cross, v)


def is_short(ref):
    kinds = ref[0, 0, 6:7]
    for z in range(ref.shape[0]):
        for y in range(NY):
            kinds = jnp.maximum(kinds, ref[z, y, 6:7])
    lane = lax.broadcasted_iota(jnp.int32, (1, SLOTS), 1)
    return jnp.max(jnp.where(lane < SHORT, -1.0, kinds)) < 0.0


def pair_body(stage, steps, home_ref, far_refs, left_ref, table_ref, before_ref,
              matrix_before_ref, out_ref, matrix_ref, gram_ref, frame_ref, lhs_ref, feat_ref,
              acc_ref, own_ref, moved_ref, moment_ref, kind_ref):
    row = sublane()
    lane = lax.broadcasted_iota(jnp.int32, (8, SLOTS), 1)
    quarter = lane // SHORT
    both = jnp.logical_and
    no = jnp.logical_not

    def far_bead(i, z, ye):
        y = lax.rem(ye + 5, 6)
        return framed(
            far_refs[i][z, y], row, steps[i] - 0.5, (ye - 4).astype(f32), (z - 3).astype(f32)
        )

    def home_bead(z, y):
        return framed(home_ref[z, y], row, -0.5, (y - 3).astype(f32), (z - 2).astype(f32))

    def prepare_whole(i):
        @pl.loop(0, 48, unroll=4)
        def _(n):
            far_features(far_bead(i, n // 8, n % 8), lhs_ref, feat_ref, i * 48 + n)

    def prepare_short(i):
        @pl.loop(0, 12, unroll=2)
        def _(n):
            v = far_bead(i, n // 2, n % 2 * 4)
            for j in range(1, 4):
                other = pltpu.roll(far_bead(i, n // 2, n % 2 * 4 + j), SHORT * j, 1)
                v = jnp.where(quarter == j, other, v)
            far_features(v, lhs_ref, feat_ref, i * 48 + n // 2 * 8 + n % 2)

    def prepare_home():
        @pl.loop(0, HOMES, unroll=4)
        def _(h):
            home_features(home_bead(h // 6, h % 6), gram_ref, frame_ref, h)

    def prepare_packed():
        @pl.loop(0, 2 * ZC, unroll=2)
        def _(n):
            z = n // 2
            y = n % 2 * 3
            v = home_bead(z, y)
            for j in (1, 2):
                v = jnp.where(quarter == j, pltpu.roll(home_bead(z, y + j), SHORT * j, 1), v)
            v = jnp.where(quarter == 3, jnp.where(row == 6, -1.0, 0.0), v)
            home_features(v, gram_ref, frame_ref, HOMES + n)

    def gather(h, slots, target_ref):
        gram = gram_ref[h]
        acc = None
        for slot in slots:
            g = jnp.dot(lhs_ref[slot, :, 0:48], gram, preferred_element_type=f32)
            e = jnp.maximum(g[:, :SLOTS], 0.0)
            terms = jnp.concatenate([e * e, e * g[:, SLOTS:]], axis=1)
            high = terms.astype(bf16)
            low = (terms - high.astype(f32)).astype(bf16)
            feat = feat_ref[slot]
            part = jnp.dot(
                jnp.concatenate([feat, feat], axis=1),
                jnp.concatenate([high, low], axis=0),
                preferred_element_type=f32,
            )
            if stage == 0 and acc is None:
                own_ref[h] = part[56:, :SLOTS]
            acc = part if acc is None else acc + part
        target_ref[h] = acc

    def gather_homes(group, tiles, target_ref):
        @pl.loop(0, HOMES // group)
        def _(q):
            for j in range(group):
                h = q * group + j
                z = h // 6
                y = h % 6
                gather(h, [(i * 6 + z + dz) * 8 + y + dy for i, dz, dy in tiles], target_ref)

    def gather_short(i, tiles):
        @pl.loop(0, ZC)
        def _(z):
            for y in range(NY):
                slots = [(z + dz) * 8 + y + dy for _, dz, dy in tiles]
                for dz in range(3):
                    for half in range(y // 4, (y + 2) // 4 + 1):
                        slots.append((i * 6 + z + dz) * 8 + half)
                gather(z * 6 + y, slots, acc_ref)

    def gather_packed(i, short):
        @pl.loop(0, ZC)
        def _(z):
            for t in range(2):
                cells = range(2) if short else range(3 * t, 3 * t + 5)
                slots = [(i * 6 + z + dz) * 8 + c for dz in range(3) for c in cells]
                gather(HOMES + 2 * z + t, slots, acc_ref)

    if stage == 0:
        prepare_whole(0)
        prepare_home()
        gather_homes(4, OWN_HALF, acc_ref)
    else:
        home_short = is_short(home_ref)
        left_short = is_short(left_ref)
        right_short = is_short(far_refs[1])
        moves = both(both(no(home_short), left_short), no(right_short))
        pl.when(home_short)(prepare_packed)
    if stage == 1:
        pl.when(left_short)(lambda: prepare_short(0))
        pl.when(no(left_short))(lambda: prepare_whole(0))
        pl.when(moves)(lambda: prepare_whole(1))
        pl.when(no(home_short))(prepare_home)
        pl.when(both(home_short, left_short))(lambda: gather_packed(0, True))
        pl.when(both(home_short, no(left_short)))(lambda: gather_packed(0, False))
        pl.when(both(no(home_short), left_short))(lambda: gather_short(0, []))
        pl.when(both(no(home_short), no(left_short)))(lambda: gather_homes(3, whole(0), acc_ref))
        pl.when(moves)(lambda: gather_homes(4, MOVED, moved_ref))
        moment_ref[...] = jnp.zeros_like(moment_ref)
        kind_ref[...] = jnp.zeros_like(kind_ref)
    if stage == 2:
        prepare_whole(0)
        pl.when(right_short)(lambda: prepare_short(1))
        pl.when(no(right_short))(lambda: prepare_whole(1))
        prepare_home()
        pl.when(home_short)(lambda: gather_homes(6, OWN_OTHER, acc_ref))
        pl.when(both(home_short, right_short))(lambda: gather_packed(1, True))
        pl.when(both(home_short, no(right_short)))(lambda: gather_packed(1, False))
        pl.when(both(no(home_short), right_short))(lambda: gather_short(1, OWN_OTHER))
        pl.when(moves)(lambda: gather_homes(3, OWN_OTHER + STAYED, acc_ref))
        pl.when(both(both(no(home_short), no(left_short)), no(right_short)))(
            lambda: gather_homes(2, OWN_OTHER + whole(1), acc_ref)
        )

    table = table_ref[...]
    columns = [jnp.broadcast_to(table[:, s : s + 1], (8, SLOTS)) for s in range(KINDS)]

    def finish(h, m, moved):
        v = frame_ref[h]
        code = v[6:7]
        mix = jnp.zeros((8, SLOTS), f32)
        for s in range(KINDS):
            mix = jnp.where(code == float(s), columns[s], mix)

        def part(f, half):
            return acc_ref[h, 8 * f : 8 * f + 8, half * SLOTS : (half + 1) * SLOTS]

        def every(f, half):
            value = part(f, half)
            if moved:
                value = value + moved_ref[h, 8 * f : 8 * f + 8, half * SLOTS : (half + 1) * SLOTS]
            return value

        def mixed(value):
            return jnp.sum(value * mix, axis=0, keepdims=True)

        def away(f):
            if stage == 0:
                return part(f, 0) - own_ref[h, 8 * f - 56 : 8 * f - 48]
            return part(f, 0)

        c1 = mixed(every(0, 0))
        c2 = mixed(every(0, 1))
        rows = []
        for k in range(3):
            stretch = v[3 + k : 4 + k] * c1 - mixed(every(7 + k, 0) + every(10 + k, 0))
            bend = v[k : k + 1] * c2 - mixed(every(1 + k, 1) + every(4 + k, 1))
            rows.append(step_size * (6.0 * stretch - 24.0 * bend))
        if stage < 2:
            moment = v[7:8] * part(0, 0) + (away(13) + away(14) + away(15))
            for k in range(3):
                moment = moment - v[3 + k : 4 + k] * (part(1 + k, 0) + part(4 + k, 0))
                moment = moment - v[k : k + 1] * (away(7 + k) + away(10 + k))
            moment_ref[m] = moment
            kind_ref[m] = jnp.where(code == row.astype(f32), 1.0, 0.0)
        return rows

    def finish_homes(moved):
        @pl.loop(0, HOMES, unroll=4)
        def _(h):
            z = h // 6
            y = h % 6
            rows = finish(h, h, moved)
            for k in range(3):
                if stage == 2:
                    out_ref[k, 0, y, pl.ds(z, 1), :] = rows[k] + before_ref[z, y, k : k + 1]
                else:
                    old = frame_ref[h, 3 + k : 4 + k] if stage == 0 else before_ref[z, y, k : k + 1]
                    out_ref[z, y, k : k + 1] = rows[k] + old

    def finish_packed():
        @pl.loop(0, ZC)
        def _(z):
            for t in range(2):
                rows = finish(HOMES + 2 * z + t, 2 * z + t, False)
                for j in range(3):
                    y = 3 * t + j
                    for k in range(3):
                        value = pltpu.roll(rows[k], (SLOTS - SHORT * j) % SLOTS, 1) if j else rows[k]
                        value = jnp.where(lane[0:1] < SHORT, value, 0.0)
                        if stage == 2:
                            out_ref[k, 0, y, pl.ds(z, 1), :] += value
                        else:
                            out_ref[z, y, k : k + 1] = before_ref[z, y, k : k + 1] + value

    if stage == 0:
        finish_homes(False)
    elif stage == 1:
        pl.when(moves)(lambda: finish_homes(True))
        pl.when(both(no(home_short), no(moves)))(lambda: finish_homes(False))
        pl.when(home_short)(finish_packed)
    else:
        finish_homes(False)
        pl.when(home_short)(finish_packed)

    if stage < 2:
        total = jnp.zeros((8, 8), f32)
        moments = jnp.concatenate([moment_ref[h] for h in range(HOMES)], axis=1)
        kinds = jnp.concatenate([kind_ref[h] for h in range(HOMES)], axis=1).astype(bf16)
        for piece in pieces(moments):
            total = total + lax.dot_general(
                piece.astype(bf16), kinds, (((1,), (1,)), ((), ())), preferred_element_type=f32
            )
        if stage == 1:
            total = total + matrix_before_ref[...]
        matrix_ref[...] = total


def pair_call(stage, steps, home, fars, table, left=None, before=None, matrix_before=None):
    count = len(steps)
    feats = 112 if stage == 2 else 128
    vmem = pl.BlockSpec(memory_space=pltpu.VMEM)
    operands = [home, *fars, table]
    if stage == 2:
        operands.append(left)
    if stage > 0:
        operands.append(before)
    if stage == 1:
        operands.append(matrix_before)
    packed = HOMES if stage == 0 else HOMES + 2 * ZC
    scratch = [
        pltpu.VMEM((packed, 48, 2 * SLOTS), bf16),
        pltpu.VMEM((packed, 8, SLOTS), f32),
        pltpu.VMEM((48 * count, SLOTS, SLOTS), bf16),
        pltpu.VMEM((48 * count, feats, SLOTS), bf16),
        pltpu.VMEM((packed, feats, 2 * SLOTS), f32),
    ]
    if stage == 0:
        scratch.append(pltpu.VMEM((HOMES, 72, SLOTS), f32))
    if stage == 1:
        scratch.append(pltpu.VMEM((HOMES, feats, 2 * SLOTS), f32))
    if stage < 2:
        scratch += [pltpu.VMEM((HOMES, 8, SLOTS), f32)] * 2

    def body(home_ref, *refs):
        far_refs = refs[:count]
        table_ref = refs[count]
        refs = list(refs[count + 1 :])
        left_ref = refs.pop(0) if stage == 2 else far_refs[0]
        before_ref = refs.pop(0) if stage > 0 else None
        matrix_before_ref = refs.pop(0) if stage == 1 else None
        out_ref = refs.pop(0)
        matrix_ref = refs.pop(0) if stage < 2 else None
        main = refs[:5]
        own_ref = refs[5] if stage == 0 else None
        moved_ref = refs[5] if stage == 1 else None
        sums = refs[6:] if stage < 2 else [None] * 2
        pair_body(stage, steps, home_ref, far_refs, left_ref, table_ref, before_ref,
                  matrix_before_ref, out_ref, matrix_ref, *main, own_ref, moved_ref, *sums)

    if stage == 2:
        out = (jax.ShapeDtypeStruct((3, 1, NY, ZC, SLOTS), f32),)
    else:
        out = (
            jax.ShapeDtypeStruct((ZC, NY, 8, SLOTS), f32),
            jax.ShapeDtypeStruct((8, 8), f32),
        )
    return pl.pallas_call(
        body,
        out_shape=out,
        in_specs=[vmem] * len(operands),
        out_specs=(vmem,) * len(out),
        scratch_shapes=scratch,
        compiler_params=pltpu.CompilerParams(vmem_limit_bytes=48 * 2**20),
        name=("pairs_own", "pairs_left", "pairs_rest")[stage],
    )(*operands)


def pack_body(counts_ref, pos_ref, cot_ref, species_ref, out_ref, low_ref, high_ref):
    lane = lax.broadcasted_iota(jnp.int32, (1, SLOTS), 1)
    for y in range(NY):
        for z in range(ZC):
            rows = [pos_ref[k, 0, y, z : z + 1, :] for k in range(3)]
            rows += [cot_ref[k, 0, y, z : z + 1, :] for k in range(3)]
            kind = jnp.where(lane < counts_ref[0, z, y], species_ref[0, y, z : z + 1, :], -1)
            rows += [kind.astype(f32), jnp.zeros((1, SLOTS), f32)]
            packed = jnp.concatenate(rows, axis=0)
            out_ref[z, y] = packed
            if z == 0:
                low_ref[0, y] = packed
            if z == ZC - 1:
                high_ref[0, y] = packed


def pack(counts, positions, cotangent, species):
    vmem = pl.BlockSpec(memory_space=pltpu.VMEM)
    return pl.pallas_call(
        pack_body,
        out_shape=(
            jax.ShapeDtypeStruct((ZC, NY, 8, SLOTS), f32),
            jax.ShapeDtypeStruct((1, NY, 8, SLOTS), f32),
            jax.ShapeDtypeStruct((1, NY, 8, SLOTS), f32),
        ),
        in_specs=[pl.BlockSpec(memory_space=pltpu.SMEM)] + [vmem] * 3,
        out_specs=(vmem,) * 3,
        name="pack",
    )(counts, positions, cotangent, species)


def move(block, dx, dz):
    pairs = []
    for i in range(NX):
        for j in range(NZ):
            pairs.append((i * NZ + j, (i + dx) % NX * NZ + (j + dz) % NZ))
    return lax.ppermute(block, AXES, pairs)


OWN_HALF = [(0, 1, 1), (0, 1, 2), (0, 2, 0), (0, 2, 1), (0, 2, 2)]
OWN_OTHER = [(0, 1, 0), (0, 0, 0), (0, 0, 1), (0, 0, 2)]


MOVED = [(1, 0, 0), (1, 0, 1), (1, 0, 2), (1, 1, 0), (1, 1, 1)]
STAYED = [(1, 1, 2), (1, 2, 0), (1, 2, 1), (1, 2, 2)]


def whole(i):
    return [(i, dz, dy) for dz in range(3) for dy in range(3)]


def per_device(positions, cotangent, species, counts, amplitude):
    table = 0.5 * (amplitude + amplitude.T)
    home, low, high = pack(jnp.swapaxes(counts, 1, 2), positions, cotangent, species)
    below = move(high, 0, 1)
    above = move(low, 0, -1)
    column = jnp.concatenate([below, home, above], axis=0)
    left = move(column, 1, 0)
    right = move(column, -1, 0)
    part, matrix = pair_call(0, (0.0,), home, (column,), table)
    part, matrix = pair_call(
        1, (-1.0, 1.0), home, (left, right), table, before=part, matrix_before=matrix
    )
    sent = jnp.broadcast_to(matrix.reshape(1, KINDS * KINDS), (NX * NZ, KINDS * KINDS))
    sent, part = lax.optimization_barrier((sent, part))
    heard = lax.all_to_all(sent, AXES, 0, 0, tiled=True)
    (out,) = pair_call(2, (0.0, 1.0), home, (column, right), table, left=left, before=part)
    heard, out = lax.optimization_barrier((heard, out))
    matrix = jnp.sum(heard, axis=0).reshape(KINDS, KINDS)
    cells_total = NX * NY * NZ * ZC
    total = 6.0 * (matrix + matrix.T)
    return out, step_size * total / (2.0 * math.sqrt(cells_total / SLOTS))


def solution(mesh):
    finer = Mesh(mesh.devices.reshape(2, 8, 2, 2, 4), AXES)
    in_specs = (
        P(None, COL, None, ROW, None),
        P(None, COL, None, ROW, None),
        P(COL, None, ROW, None),
        P(COL, None, ROW),
        P(),
    )
    return jax.shard_map(
        per_device,
        mesh=finer,
        in_specs=in_specs,
        out_specs=(P(None, COL, None, ROW, None), P()),
        check_vma=False,
    )
```

```python
import math

import jax
import jax.numpy as jnp
from jax import lax
from jax.experimental import pallas as pl
from jax.experimental.pallas import tpu as pltpu
from jax.sharding import Mesh
from jax.sharding import PartitionSpec as P

AXES = ("y_hi", "z_ax", "core", "y_lo", "x_ax")
ROW = ("y_lo", "x_ax")
COL = ("y_hi", "z_ax", "core")
NX, NZ = 32, 8
step_size = 0.05
FAR = 1.0e4
NY = 6
ZC = 4
SLOTS = 128
KINDS = 8
SHORT = 32
HOMES = NY * ZC
bf16 = jnp.bfloat16
f32 = jnp.float32


def sublane(shape=(8, SLOTS)):
    return lax.broadcasted_iota(jnp.int32, shape, 0)


def pieces(v):
    high = v.astype(bf16).astype(f32)
    rest = v - high
    mid = rest.astype(bf16).astype(f32)
    return high, mid, rest - mid


def pick(row, lo, hi, value, other):
    return jnp.where((row >= lo) & (row < hi), value, other)


def row_sum(row, lo, hi, value):
    return jnp.sum(pick(row, lo, hi, value, 0.0), axis=0, keepdims=True)


def framed(raw, row, sx, sy, sz):
    shift = jnp.where(row == 0, sx, jnp.where(row == 1, sy, jnp.where(row == 2, sz, 0.0)))
    return raw + shift.astype(f32)


def bead_terms(v, row):
    back = pltpu.roll(v, 3, 0)
    square = row_sum(row, 0, 3, v * v)
    cross = row_sum(row, 3, 6, v * back)
    return back, square, cross


def far_features(v, lhs_ref, feat_ref, slot):
    row = sublane()
    back, square, cross = bead_terms(v, row)
    code = v[6:7]
    ahead = pltpu.roll(v, 5, 0)
    gain = jnp.where(code < 0.0, -FAR, 1.0 - square)
    a = pick(row, 0, 3, ahead, pick(row, 3, 6, back, 0.0))
    ah, am, al = pieces(a)
    qh, qm, ql = pieces(gain)
    rh, rm, rl = pieces(cross)
    one = jnp.where(row == 6, 1.0, 0.0)
    last = row == 7
    lhs = jnp.concatenate(
        [
            jnp.where(last, qh, ah + one),
            jnp.where(last, qm, ah + one),
            jnp.where(last, ql, ah + one),
            jnp.where(last, rh, am),
            jnp.where(last, rm, am),
            jnp.where(last, rl, al),
        ],
        axis=0,
    )
    lhs_ref[slot, :, 0:48] = lhs.astype(bf16).T
    mask = code == row.astype(f32)
    high = v.astype(bf16).astype(f32)
    low = v - high
    rows = [jnp.where(mask, 1.0, 0.0)]
    for part, start in ((high, 0), (low, 0), (high, 3), (low, 3)):
        for k in range(3):
            rows.append(jnp.where(mask, part[start + k : start + k + 1], 0.0))
    if feat_ref.shape[1] == 128:
        rows += [jnp.where(mask, r, 0.0) for r in (rh, rm, rl)]
    else:
        rows.append(jnp.zeros((8, SLOTS), f32))
    feat_ref[slot] = jnp.concatenate(rows, axis=0).astype(bf16)


def home_features(v, gram_ref, frame_ref, h):
    row = sublane()
    back, square, cross = bead_terms(v, row)
    square = jnp.where(v[6:7] < 0.0, FAR, square)
    u = pick(row, 3, 6, 2.0 * back, jnp.where(row == 6, -square, 0.0))
    p = pick(row, 0, 6, -v, jnp.where(row == 6, cross, 0.0))
    last = jnp.where(row == 7, 1.0, 0.0)
    uh, um, ul = pieces(u)
    ph, pm, pl_ = pieces(p)
    gram_ref[h, :, 0:SLOTS] = jnp.concatenate(
        [uh + last, um + last, ul + last, uh, um, uh], axis=0
    ).astype(bf16)
    gram_ref[h, :, SLOTS : 2 * SLOTS] = jnp.concatenate(
        [ph, pm, pl_, ph + last, pm + last, ph + last], axis=0
    ).astype(bf16)
    frame_ref[h] = jnp.where(row == 7, cross, v)


def is_short(ref):
    kinds = ref[0, 0, 6:7]
    for z in range(ref.shape[0]):
        for y in range(NY):
            kinds = jnp.maximum(kinds, ref[z, y, 6:7])
    lane = lax.broadcasted_iota(jnp.int32, (1, SLOTS), 1)
    return jnp.max(jnp.where(lane < SHORT, -1.0, kinds)) < 0.0


def pair_body(stage, steps, home_ref, far_refs, left_ref, table_ref, before_ref,
              matrix_before_ref, out_ref, matrix_ref, gram_ref, frame_ref, lhs_ref, feat_ref,
              acc_ref, own_ref, moved_ref, moment_ref, kind_ref):
    row = sublane()
    lane = lax.broadcasted_iota(jnp.int32, (8, SLOTS), 1)
    quarter = lane // SHORT
    both = jnp.logical_and
    no = jnp.logical_not

    def far_bead(i, z, ye):
        y = lax.rem(ye + 5, 6)
        return framed(
            far_refs[i][z, y], row, steps[i] - 0.5, (ye - 4).astype(f32), (z - 3).astype(f32)
        )

    def home_bead(z, y):
        return framed(home_ref[z, y], row, -0.5, (y - 3).astype(f32), (z - 2).astype(f32))

    def prepare_whole(i, low=0, high=6):
        @pl.loop(8 * low, 8 * high, unroll=4)
        def _(n):
            far_features(far_bead(i, n // 8, n % 8), lhs_ref, feat_ref, i * 48 + n)

    def prepare_short(i):
        @pl.loop(0, 12, unroll=2)
        def _(n):
            v = far_bead(i, n // 2, n % 2 * 4)
            for j in range(1, 4):
                other = pltpu.roll(far_bead(i, n // 2, n % 2 * 4 + j), SHORT * j, 1)
                v = jnp.where(quarter == j, other, v)
            far_features(v, lhs_ref, feat_ref, i * 48 + n // 2 * 8 + n % 2)

    def prepare_home():
        @pl.loop(0, HOMES, unroll=4)
        def _(h):
            home_features(home_bead(h // 6, h % 6), gram_ref, frame_ref, h)

    def prepare_packed():
        @pl.loop(0, 2 * ZC, unroll=2)
        def _(n):
            z = n // 2
            y = n % 2 * 3
            v = home_bead(z, y)
            for j in (1, 2):
                v = jnp.where(quarter == j, pltpu.roll(home_bead(z, y + j), SHORT * j, 1), v)
            v = jnp.where(quarter == 3, jnp.where(row == 6, -1.0, 0.0), v)
            home_features(v, gram_ref, frame_ref, HOMES + n)

    def gather(h, slots, target_ref):
        gram = gram_ref[h]
        acc = None
        for slot in slots:
            g = jnp.dot(lhs_ref[slot, :, 0:48], gram, preferred_element_type=f32)
            e = jnp.maximum(g[:, :SLOTS], 0.0)
            terms = jnp.concatenate([e * e, e * g[:, SLOTS:]], axis=1)
            high = terms.astype(bf16)
            low = (terms - high.astype(f32)).astype(bf16)
            feat = feat_ref[slot]
            part = jnp.dot(
                jnp.concatenate([feat, feat], axis=1),
                jnp.concatenate([high, low], axis=0),
                preferred_element_type=f32,
            )
            if stage == 0 and acc is None:
                own_ref[h] = part[56:, :SLOTS]
            acc = part if acc is None else acc + part
        target_ref[h] = acc

    def gather_homes(group, tiles, target_ref, first=0, last=HOMES):
        @pl.loop(0, (last - first) // group)
        def _(q):
            for j in range(group):
                h = first + q * group + j
                z = h // 6
                y = h % 6
                gather(h, [(i * 6 + z + dz) * 8 + y + dy for i, dz, dy in tiles], target_ref)

    def gather_short(i, tiles):
        @pl.loop(0, ZC)
        def _(z):
            for y in range(NY):
                slots = [(z + dz) * 8 + y + dy for _, dz, dy in tiles]
                for dz in range(3):
                    for half in range(y // 4, (y + 2) // 4 + 1):
                        slots.append((i * 6 + z + dz) * 8 + half)
                gather(z * 6 + y, slots, acc_ref)

    def gather_packed(i, short, depths, target_ref):
        @pl.loop(0, ZC // 2)
        def _(pair):
            for z in (2 * pair, 2 * pair + 1):
                for t in range(2):
                    cells = range(2) if short else range(3 * t, 3 * t + 5)
                    slots = [(i * 6 + z + dz) * 8 + c for dz in depths for c in cells]
                    gather(HOMES + 2 * z + t, slots, target_ref)

    if stage == 0:
        prepare_whole(0, 1, 6)
        prepare_home()
        gather_homes(4, OWN_HALF, acc_ref)
    else:
        home_short = is_short(home_ref)
        left_short = is_short(left_ref)
        right_short = is_short(far_refs[1])
        moves = both(both(no(home_short), left_short), no(right_short))
        packed_moves = both(home_short, no(right_short))
        pl.when(home_short)(prepare_packed)
    if stage == 1:
        pl.when(left_short)(lambda: prepare_short(0))
        pl.when(no(left_short))(lambda: prepare_whole(0))
        pl.when(moves)(lambda: prepare_whole(1, 0, 4))
        pl.when(packed_moves)(lambda: prepare_whole(1, 0, 5))
        pl.when(no(home_short))(prepare_home)
        pl.when(both(home_short, left_short))(lambda: gather_packed(0, True, range(3), acc_ref))
        pl.when(both(home_short, no(left_short)))(lambda: gather_packed(0, False, range(3), acc_ref))
        pl.when(both(no(home_short), left_short))(lambda: gather_short(0, []))
        pl.when(both(no(home_short), no(left_short)))(lambda: gather_homes(3, whole(0), acc_ref))
        pl.when(moves)(lambda: gather_homes(3, whole(1), moved_ref, 0, HOMES // 2))
        pl.when(packed_moves)(lambda: gather_packed(1, False, (0, 1), moved_ref))
        moment_ref[...] = jnp.zeros_like(moment_ref)
        kind_ref[...] = jnp.zeros_like(kind_ref)
    if stage == 2:
        prepare_whole(0, 0, 5)
        pl.when(right_short)(lambda: prepare_short(1))
        partly = jnp.logical_or(moves, packed_moves)
        pl.when(partly)(lambda: prepare_whole(1, 2, 6))
        pl.when(no(jnp.logical_or(partly, right_short)))(lambda: prepare_whole(1))
        prepare_home()
        pl.when(home_short)(lambda: gather_homes(6, OWN_OTHER, acc_ref))
        pl.when(both(home_short, right_short))(lambda: gather_packed(1, True, range(3), acc_ref))
        pl.when(packed_moves)(lambda: gather_packed(1, False, (2,), acc_ref))
        pl.when(both(no(home_short), right_short))(lambda: gather_short(1, OWN_OTHER))

        @pl.when(moves)
        def _():
            gather_homes(6, OWN_OTHER, acc_ref, 0, HOMES // 2)
            gather_homes(2, OWN_OTHER + whole(1), acc_ref, HOMES // 2)

        pl.when(both(both(no(home_short), no(left_short)), no(right_short)))(
            lambda: gather_homes(2, OWN_OTHER + whole(1), acc_ref)
        )

    table = table_ref[...]
    columns = [jnp.broadcast_to(table[:, s : s + 1], (8, SLOTS)) for s in range(KINDS)]

    def finish(h, m, moved):
        v = frame_ref[h]
        code = v[6:7]
        mix = jnp.zeros((8, SLOTS), f32)
        for s in range(KINDS):
            mix = jnp.where(code == float(s), columns[s], mix)

        def part(f, half):
            return acc_ref[h, 8 * f : 8 * f + 8, half * SLOTS : (half + 1) * SLOTS]

        def every(f, half):
            value = part(f, half)
            if moved:
                value = value + moved_ref[h, 8 * f : 8 * f + 8, half * SLOTS : (half + 1) * SLOTS]
            return value

        def mixed(value):
            return jnp.sum(value * mix, axis=0, keepdims=True)

        def away(f):
            if stage == 0:
                return part(f, 0) - own_ref[h, 8 * f - 56 : 8 * f - 48]
            return part(f, 0)

        c1 = mixed(every(0, 0))
        c2 = mixed(every(0, 1))
        rows = []
        for k in range(3):
            stretch = v[3 + k : 4 + k] * c1 - mixed(every(7 + k, 0) + every(10 + k, 0))
            bend = v[k : k + 1] * c2 - mixed(every(1 + k, 1) + every(4 + k, 1))
            rows.append(step_size * (6.0 * stretch - 24.0 * bend))
        if stage < 2:
            moment = v[7:8] * part(0, 0) + (away(13) + away(14) + away(15))
            for k in range(3):
                moment = moment - v[3 + k : 4 + k] * (part(1 + k, 0) + part(4 + k, 0))
                moment = moment - v[k : k + 1] * (away(7 + k) + away(10 + k))
            moment_ref[m] = moment
            kind_ref[m] = jnp.where(code == row.astype(f32), 1.0, 0.0)
        return rows

    def finish_homes(moved, first=0, last=HOMES):
        @pl.loop(first, last, unroll=4)
        def _(h):
            z = h // 6
            y = h % 6
            rows = finish(h, h, moved)
            for k in range(3):
                if stage == 2:
                    out_ref[k, 0, y, pl.ds(z, 1), :] = rows[k] + before_ref[z, y, k : k + 1]
                else:
                    old = frame_ref[h, 3 + k : 4 + k] if stage == 0 else before_ref[z, y, k : k + 1]
                    out_ref[z, y, k : k + 1] = rows[k] + old

    def finish_packed(moved):
        @pl.loop(0, ZC, unroll=2)
        def _(z):
            for t in range(2):
                rows = finish(HOMES + 2 * z + t, 2 * z + t, moved)
                for j in range(3):
                    y = 3 * t + j
                    for k in range(3):
                        value = pltpu.roll(rows[k], (SLOTS - SHORT * j) % SLOTS, 1) if j else rows[k]
                        value = jnp.where(lane[0:1] < SHORT, value, 0.0)
                        if stage == 2:
                            out_ref[k, 0, y, pl.ds(z, 1), :] += value
                        else:
                            out_ref[z, y, k : k + 1] = before_ref[z, y, k : k + 1] + value

    if stage == 0:
        finish_homes(False)
    elif stage == 1:
        pl.when(moves)(lambda: finish_homes(True, 0, HOMES // 2))
        pl.when(moves)(lambda: finish_homes(False, HOMES // 2))
        pl.when(both(no(home_short), no(moves)))(lambda: finish_homes(False))
        pl.when(packed_moves)(lambda: finish_packed(True))
        pl.when(both(home_short, right_short))(lambda: finish_packed(False))
    else:
        finish_homes(False)
        pl.when(home_short)(lambda: finish_packed(False))

    if stage < 2:
        total = jnp.zeros((8, 8), f32)
        moments = jnp.concatenate([moment_ref[h] for h in range(HOMES)], axis=1)
        kinds = jnp.concatenate([kind_ref[h] for h in range(HOMES)], axis=1).astype(bf16)
        for piece in pieces(moments):
            total = total + lax.dot_general(
                piece.astype(bf16), kinds, (((1,), (1,)), ((), ())), preferred_element_type=f32
            )
        if stage == 1:
            total = total + matrix_before_ref[...]
        matrix_ref[...] = total


def pair_call(stage, steps, home, fars, table, left=None, before=None, matrix_before=None):
    count = len(steps)
    feats = 112 if stage == 2 else 128
    vmem = pl.BlockSpec(memory_space=pltpu.VMEM)
    operands = [home, *fars, table]
    if stage == 2:
        operands.append(left)
    if stage > 0:
        operands.append(before)
    if stage == 1:
        operands.append(matrix_before)
    packed = HOMES if stage == 0 else HOMES + 2 * ZC
    scratch = [
        pltpu.VMEM((packed, 48, 2 * SLOTS), bf16),
        pltpu.VMEM((packed, 8, SLOTS), f32),
        pltpu.VMEM((48 * count, SLOTS, SLOTS), bf16),
        pltpu.VMEM((48 * count, feats, SLOTS), bf16),
        pltpu.VMEM((packed, feats, 2 * SLOTS), f32),
    ]
    if stage == 0:
        scratch.append(pltpu.VMEM((HOMES, 72, SLOTS), f32))
    if stage == 1:
        scratch.append(pltpu.VMEM((packed, feats, 2 * SLOTS), f32))
    if stage < 2:
        scratch += [pltpu.VMEM((HOMES, 8, SLOTS), f32)] * 2

    def body(home_ref, *refs):
        far_refs = refs[:count]
        table_ref = refs[count]
        refs = list(refs[count + 1 :])
        left_ref = refs.pop(0) if stage == 2 else far_refs[0]
        before_ref = refs.pop(0) if stage > 0 else None
        matrix_before_ref = refs.pop(0) if stage == 1 else None
        out_ref = refs.pop(0)
        matrix_ref = refs.pop(0) if stage < 2 else None
        main = refs[:5]
        own_ref = refs[5] if stage == 0 else None
        moved_ref = refs[5] if stage == 1 else None
        sums = refs[6:] if stage < 2 else [None] * 2
        pair_body(stage, steps, home_ref, far_refs, left_ref, table_ref, before_ref,
                  matrix_before_ref, out_ref, matrix_ref, *main, own_ref, moved_ref, *sums)

    if stage == 2:
        out = (jax.ShapeDtypeStruct((3, 1, NY, ZC, SLOTS), f32),)
    else:
        out = (
            jax.ShapeDtypeStruct((ZC, NY, 8, SLOTS), f32),
            jax.ShapeDtypeStruct((8, 8), f32),
        )
    return pl.pallas_call(
        body,
        out_shape=out,
        in_specs=[vmem] * len(operands),
        out_specs=(vmem,) * len(out),
        scratch_shapes=scratch,
        compiler_params=pltpu.CompilerParams(vmem_limit_bytes=48 * 2**20),
        name=("pairs_own", "pairs_left", "pairs_rest")[stage],
    )(*operands)


def pack_body(counts_ref, pos_ref, cot_ref, species_ref, out_ref, low_ref, high_ref):
    lane = lax.broadcasted_iota(jnp.int32, (1, SLOTS), 1)
    for y in range(NY):
        for z in range(ZC):
            rows = [pos_ref[k, 0, y, z : z + 1, :] for k in range(3)]
            rows += [cot_ref[k, 0, y, z : z + 1, :] for k in range(3)]
            kind = jnp.where(lane < counts_ref[0, z, y], species_ref[0, y, z : z + 1, :], -1)
            rows += [kind.astype(f32), jnp.zeros((1, SLOTS), f32)]
            packed = jnp.concatenate(rows, axis=0)
            out_ref[z, y] = packed
            if z == 0:
                low_ref[0, y] = packed
            if z == ZC - 1:
                high_ref[0, y] = packed


def pack(counts, positions, cotangent, species):
    vmem = pl.BlockSpec(memory_space=pltpu.VMEM)
    return pl.pallas_call(
        pack_body,
        out_shape=(
            jax.ShapeDtypeStruct((ZC, NY, 8, SLOTS), f32),
            jax.ShapeDtypeStruct((1, NY, 8, SLOTS), f32),
            jax.ShapeDtypeStruct((1, NY, 8, SLOTS), f32),
        ),
        in_specs=[pl.BlockSpec(memory_space=pltpu.SMEM)] + [vmem] * 3,
        out_specs=(vmem,) * 3,
        name="pack",
    )(counts, positions, cotangent, species)


def move(block, dx, dz):
    pairs = []
    for i in range(NX):
        for j in range(NZ):
            pairs.append((i * NZ + j, (i + dx) % NX * NZ + (j + dz) % NZ))
    return lax.ppermute(block, AXES, pairs)


OWN_HALF = [(0, 1, 1), (0, 1, 2), (0, 2, 0), (0, 2, 1), (0, 2, 2)]
OWN_OTHER = [(0, 1, 0), (0, 0, 0), (0, 0, 1), (0, 0, 2)]


def whole(i):
    return [(i, dz, dy) for dz in range(3) for dy in range(3)]


def per_device(positions, cotangent, species, counts, amplitude):
    table = 0.5 * (amplitude + amplitude.T)
    home, low, high = pack(jnp.swapaxes(counts, 1, 2), positions, cotangent, species)
    below = move(high, 0, 1)
    above = move(low, 0, -1)
    column = jnp.concatenate([below, home, above], axis=0)
    left = move(column, 1, 0)
    right = move(column, -1, 0)
    part, matrix = pair_call(0, (0.0,), home, (column,), table)
    part, matrix = pair_call(
        1, (-1.0, 1.0), home, (left, right), table, before=part, matrix_before=matrix
    )
    sent = jnp.broadcast_to(matrix.reshape(1, KINDS * KINDS), (NX * NZ, KINDS * KINDS))
    sent, part = lax.optimization_barrier((sent, part))
    heard = lax.all_to_all(sent, AXES, 0, 0, tiled=True)
    (out,) = pair_call(2, (0.0, 1.0), home, (column, right), table, left=left, before=part)
    heard, out = lax.optimization_barrier((heard, out))
    matrix = jnp.sum(heard, axis=0).reshape(KINDS, KINDS)
    cells_total = NX * NY * NZ * ZC
    total = 6.0 * (matrix + matrix.T)
    return out, step_size * total / (2.0 * math.sqrt(cells_total / SLOTS))


def solution(mesh):
    finer = Mesh(mesh.devices.reshape(2, 8, 2, 2, 4), AXES)
    in_specs = (
        P(None, COL, None, ROW, None),
        P(None, COL, None, ROW, None),
        P(COL, None, ROW, None),
        P(COL, None, ROW),
        P(),
    )
    return jax.shard_map(
        per_device,
        mesh=finer,
        in_specs=in_specs,
        out_specs=(P(None, COL, None, ROW, None), P()),
        check_vma=False,
    )
```

```python
import math

import jax
import jax.numpy as jnp
from jax import lax
from jax.experimental import pallas as pl
from jax.experimental.pallas import tpu as pltpu
from jax.sharding import Mesh
from jax.sharding import PartitionSpec as P

AXES = ("y_hi", "z_ax", "core", "y_lo", "x_ax")
ROW = ("y_lo", "x_ax")
COL = ("y_hi", "z_ax", "core")
NX, NZ = 32, 8
step_size = 0.05
FAR = 1.0e4
NY = 6
ZC = 4
SLOTS = 128
KINDS = 8
SHORT = 32
HOMES = NY * ZC
bf16 = jnp.bfloat16
f32 = jnp.float32


def sublane(shape=(8, SLOTS)):
    return lax.broadcasted_iota(jnp.int32, shape, 0)


def pieces(v):
    high = v.astype(bf16).astype(f32)
    rest = v - high
    mid = rest.astype(bf16).astype(f32)
    return high, mid, rest - mid


def pick(row, lo, hi, value, other):
    return jnp.where((row >= lo) & (row < hi), value, other)


def row_sum(row, lo, hi, value):
    return jnp.sum(pick(row, lo, hi, value, 0.0), axis=0, keepdims=True)


def framed(raw, row, sx, sy, sz):
    shift = jnp.where(row == 0, sx, jnp.where(row == 1, sy, jnp.where(row == 2, sz, 0.0)))
    return raw + shift.astype(f32)


def bead_terms(v, row):
    back = pltpu.roll(v, 3, 0)
    square = row_sum(row, 0, 3, v * v)
    cross = row_sum(row, 3, 6, v * back)
    return back, square, cross


def far_features(v, lhs_ref, feat_ref, slot):
    row = sublane()
    back, square, cross = bead_terms(v, row)
    code = v[6:7]
    ahead = pltpu.roll(v, 5, 0)
    gain = jnp.where(code < 0.0, -FAR, 1.0 - square)
    a = pick(row, 0, 3, ahead, pick(row, 3, 6, back, 0.0))
    ah, am, al = pieces(a)
    qh, qm, ql = pieces(gain)
    rh, rm, rl = pieces(cross)
    one = jnp.where(row == 6, 1.0, 0.0)
    last = row == 7
    lhs = jnp.concatenate(
        [
            jnp.where(last, qh, ah + one),
            jnp.where(last, qm, ah + one),
            jnp.where(last, ql, ah + one),
            jnp.where(last, rh, am),
            jnp.where(last, rm, am),
            jnp.where(last, rl, al),
        ],
        axis=0,
    )
    lhs_ref[slot, :, 0:48] = lhs.astype(bf16).T
    mask = code == row.astype(f32)
    high = v.astype(bf16).astype(f32)
    low = v - high
    rows = [jnp.where(mask, 1.0, 0.0)]
    for part, start in ((high, 0), (low, 0), (high, 3), (low, 3)):
        for k in range(3):
            rows.append(jnp.where(mask, part[start + k : start + k + 1], 0.0))
    if feat_ref.shape[1] == 128:
        rows += [jnp.where(mask, r, 0.0) for r in (rh, rm, rl)]
    else:
        rows.append(jnp.zeros((8, SLOTS), f32))
    feat_ref[slot] = jnp.concatenate(rows, axis=0).astype(bf16)


def home_features(v, gram_ref, frame_ref, h):
    row = sublane()
    back, square, cross = bead_terms(v, row)
    square = jnp.where(v[6:7] < 0.0, FAR, square)
    u = pick(row, 3, 6, 2.0 * back, jnp.where(row == 6, -square, 0.0))
    p = pick(row, 0, 6, -v, jnp.where(row == 6, cross, 0.0))
    last = jnp.where(row == 7, 1.0, 0.0)
    uh, um, ul = pieces(u)
    ph, pm, pl_ = pieces(p)
    gram_ref[h, :, 0:SLOTS] = jnp.concatenate(
        [uh + last, um + last, ul + last, uh, um, uh], axis=0
    ).astype(bf16)
    gram_ref[h, :, SLOTS : 2 * SLOTS] = jnp.concatenate(
        [ph, pm, pl_, ph + last, pm + last, ph + last], axis=0
    ).astype(bf16)
    frame_ref[h] = jnp.where(row == 7, cross, v)


def is_short(ref):
    kinds = ref[0, 0, 6:7]
    for z in range(ref.shape[0]):
        for y in range(NY):
            kinds = jnp.maximum(kinds, ref[z, y, 6:7])
    lane = lax.broadcasted_iota(jnp.int32, (1, SLOTS), 1)
    return jnp.max(jnp.where(lane < SHORT, -1.0, kinds)) < 0.0


def pair_body(stage, steps, home_ref, far_refs, left_ref, table_ref, before_ref,
              matrix_before_ref, out_ref, matrix_ref, gram_ref, frame_ref, lhs_ref, feat_ref,
              acc_ref, own_ref, moved_ref, moment_ref, kind_ref):
    row = sublane()
    lane = lax.broadcasted_iota(jnp.int32, (8, SLOTS), 1)
    quarter = lane // SHORT
    both = jnp.logical_and
    no = jnp.logical_not

    def far_bead(i, z, ye):
        y = lax.rem(ye + 5, 6)
        return framed(
            far_refs[i][z, y], row, steps[i] - 0.5, (ye - 4).astype(f32), (z - 3).astype(f32)
        )

    def home_bead(z, y):
        return framed(home_ref[z, y], row, -0.5, (y - 3).astype(f32), (z - 2).astype(f32))

    def prepare_whole(i, low=0, high=6):
        @pl.loop(8 * low, 8 * high, unroll=8)
        def _(n):
            far_features(far_bead(i, n // 8, n % 8), lhs_ref, feat_ref, i * 48 + n)

    def prepare_short(i):
        @pl.loop(0, 12, unroll=2)
        def _(n):
            v = far_bead(i, n // 2, n % 2 * 4)
            for j in range(1, 4):
                other = pltpu.roll(far_bead(i, n // 2, n % 2 * 4 + j), SHORT * j, 1)
                v = jnp.where(quarter == j, other, v)
            far_features(v, lhs_ref, feat_ref, i * 48 + n // 2 * 8 + n % 2)

    def prepare_home():
        @pl.loop(0, HOMES, unroll=8)
        def _(h):
            home_features(home_bead(h // 6, h % 6), gram_ref, frame_ref, h)

    def prepare_packed():
        @pl.loop(0, 2 * ZC, unroll=2)
        def _(n):
            z = n // 2
            y = n % 2 * 3
            v = home_bead(z, y)
            for j in (1, 2):
                v = jnp.where(quarter == j, pltpu.roll(home_bead(z, y + j), SHORT * j, 1), v)
            v = jnp.where(quarter == 3, jnp.where(row == 6, -1.0, 0.0), v)
            home_features(v, gram_ref, frame_ref, HOMES + n)

    def gather(h, slots, target_ref):
        gram = gram_ref[h]
        acc = None
        for slot in slots:
            g = jnp.dot(lhs_ref[slot, :, 0:48], gram, preferred_element_type=f32)
            e = jnp.maximum(g[:, :SLOTS], 0.0)
            terms = jnp.concatenate([e * e, e * g[:, SLOTS:]], axis=1)
            high = terms.astype(bf16)
            low = (terms - high.astype(f32)).astype(bf16)
            feat = feat_ref[slot]
            part = jnp.dot(
                jnp.concatenate([feat, feat], axis=1),
                jnp.concatenate([high, low], axis=0),
                preferred_element_type=f32,
            )
            if stage == 0 and acc is None:
                own_ref[h] = part[56:, :SLOTS]
            acc = part if acc is None else acc + part
        target_ref[h] = acc

    def gather_homes(group, tiles, target_ref, first=0, last=HOMES):
        @pl.loop(0, (last - first) // group)
        def _(q):
            for j in range(group):
                h = first + q * group + j
                z = h // 6
                y = h % 6
                gather(h, [(i * 6 + z + dz) * 8 + y + dy for i, dz, dy in tiles], target_ref)

    def gather_short(i, tiles):
        @pl.loop(0, ZC)
        def _(z):
            for y in range(NY):
                slots = [(z + dz) * 8 + y + dy for _, dz, dy in tiles]
                for dz in range(3):
                    for half in range(y // 4, (y + 2) // 4 + 1):
                        slots.append((i * 6 + z + dz) * 8 + half)
                gather(z * 6 + y, slots, acc_ref)

    def gather_packed(i, short, depths, target_ref):
        @pl.loop(0, ZC // 2)
        def _(pair):
            for z in (2 * pair, 2 * pair + 1):
                for t in range(2):
                    cells = range(2) if short else range(3 * t, 3 * t + 5)
                    slots = [(i * 6 + z + dz) * 8 + c for dz in depths for c in cells]
                    gather(HOMES + 2 * z + t, slots, target_ref)

    if stage == 0:
        prepare_whole(0, 1, 6)
        prepare_home()
        gather_homes(6, OWN_HALF, acc_ref)
    else:
        home_short = is_short(home_ref)
        left_short = is_short(left_ref)
        right_short = is_short(far_refs[1])
        moves = both(both(no(home_short), left_short), no(right_short))
        packed_moves = both(home_short, no(right_short))
        pl.when(home_short)(prepare_packed)
    if stage == 1:
        pl.when(left_short)(lambda: prepare_short(0))
        pl.when(no(left_short))(lambda: prepare_whole(0))
        pl.when(moves)(lambda: prepare_whole(1, 0, 4))
        pl.when(packed_moves)(lambda: prepare_whole(1, 0, 5))
        pl.when(no(home_short))(prepare_home)
        pl.when(both(home_short, left_short))(lambda: gather_packed(0, True, range(3), acc_ref))
        pl.when(both(home_short, no(left_short)))(lambda: gather_packed(0, False, range(3), acc_ref))
        pl.when(both(no(home_short), left_short))(lambda: gather_short(0, []))
        pl.when(both(no(home_short), no(left_short)))(lambda: gather_homes(4, whole(0), acc_ref))
        pl.when(moves)(lambda: gather_homes(3, whole(1), moved_ref, 0, HOMES // 2))
        pl.when(packed_moves)(lambda: gather_packed(1, False, (0, 1), moved_ref))
        moment_ref[...] = jnp.zeros_like(moment_ref)
        kind_ref[...] = jnp.zeros_like(kind_ref)
    if stage == 2:
        prepare_whole(0, 0, 5)
        pl.when(right_short)(lambda: prepare_short(1))
        partly = jnp.logical_or(moves, packed_moves)
        pl.when(partly)(lambda: prepare_whole(1, 2, 6))
        pl.when(no(jnp.logical_or(partly, right_short)))(lambda: prepare_whole(1))
        prepare_home()
        pl.when(home_short)(lambda: gather_homes(6, OWN_OTHER, acc_ref))
        pl.when(both(home_short, right_short))(lambda: gather_packed(1, True, range(3), acc_ref))
        pl.when(packed_moves)(lambda: gather_packed(1, False, (2,), acc_ref))
        pl.when(both(no(home_short), right_short))(lambda: gather_short(1, OWN_OTHER))

        @pl.when(moves)
        def _():
            gather_homes(6, OWN_OTHER, acc_ref, 0, HOMES // 2)
            gather_homes(2, OWN_OTHER + whole(1), acc_ref, HOMES // 2)

        pl.when(both(both(no(home_short), no(left_short)), no(right_short)))(
            lambda: gather_homes(3, OWN_OTHER + whole(1), acc_ref)
        )

    table = table_ref[...]
    columns = [jnp.broadcast_to(table[:, s : s + 1], (8, SLOTS)) for s in range(KINDS)]

    def finish(h, m, moved):
        v = frame_ref[h]
        code = v[6:7]
        mix = jnp.zeros((8, SLOTS), f32)
        for s in range(KINDS):
            mix = jnp.where(code == float(s), columns[s], mix)

        def part(f, half):
            return acc_ref[h, 8 * f : 8 * f + 8, half * SLOTS : (half + 1) * SLOTS]

        def every(f, half):
            value = part(f, half)
            if moved:
                value = value + moved_ref[h, 8 * f : 8 * f + 8, half * SLOTS : (half + 1) * SLOTS]
            return value

        def mixed(value):
            return jnp.sum(value * mix, axis=0, keepdims=True)

        def away(f):
            if stage == 0:
                return part(f, 0) - own_ref[h, 8 * f - 56 : 8 * f - 48]
            return part(f, 0)

        c1 = mixed(every(0, 0))
        c2 = mixed(every(0, 1))
        rows = []
        for k in range(3):
            stretch = v[3 + k : 4 + k] * c1 - mixed(every(7 + k, 0) + every(10 + k, 0))
            bend = v[k : k + 1] * c2 - mixed(every(1 + k, 1) + every(4 + k, 1))
            rows.append(step_size * (6.0 * stretch - 24.0 * bend))
        if stage < 2:
            moment = v[7:8] * part(0, 0) + (away(13) + away(14) + away(15))
            for k in range(3):
                moment = moment - v[3 + k : 4 + k] * (part(1 + k, 0) + part(4 + k, 0))
                moment = moment - v[k : k + 1] * (away(7 + k) + away(10 + k))
            moment_ref[m] = moment
            kind_ref[m] = jnp.where(code == row.astype(f32), 1.0, 0.0)
        return rows

    def finish_homes(moved, first=0, last=HOMES):
        @pl.loop(first, last, unroll=6)
        def _(h):
            z = h // 6
            y = h % 6
            rows = finish(h, h, moved)
            for k in range(3):
                if stage == 2:
                    out_ref[k, 0, y, pl.ds(z, 1), :] = rows[k] + before_ref[z, y, k : k + 1]
                else:
                    old = frame_ref[h, 3 + k : 4 + k] if stage == 0 else before_ref[z, y, k : k + 1]
                    out_ref[z, y, k : k + 1] = rows[k] + old

    def finish_packed(moved):
        @pl.loop(0, ZC, unroll=2)
        def _(z):
            for t in range(2):
                rows = finish(HOMES + 2 * z + t, 2 * z + t, moved)
                for j in range(3):
                    y = 3 * t + j
                    for k in range(3):
                        value = pltpu.roll(rows[k], (SLOTS - SHORT * j) % SLOTS, 1) if j else rows[k]
                        value = jnp.where(lane[0:1] < SHORT, value, 0.0)
                        if stage == 2:
                            out_ref[k, 0, y, pl.ds(z, 1), :] += value
                        else:
                            out_ref[z, y, k : k + 1] = before_ref[z, y, k : k + 1] + value

    if stage == 0:
        finish_homes(False)
    elif stage == 1:
        pl.when(moves)(lambda: finish_homes(True, 0, HOMES // 2))
        pl.when(moves)(lambda: finish_homes(False, HOMES // 2))
        pl.when(both(no(home_short), no(moves)))(lambda: finish_homes(False))
        pl.when(packed_moves)(lambda: finish_packed(True))
        pl.when(both(home_short, right_short))(lambda: finish_packed(False))
    else:
        finish_homes(False)
        pl.when(home_short)(lambda: finish_packed(False))

    if stage < 2:
        total = jnp.zeros((8, 8), f32)
        moments = jnp.concatenate([moment_ref[h] for h in range(HOMES)], axis=1)
        kinds = jnp.concatenate([kind_ref[h] for h in range(HOMES)], axis=1).astype(bf16)
        for piece in pieces(moments):
            total = total + lax.dot_general(
                piece.astype(bf16), kinds, (((1,), (1,)), ((), ())), preferred_element_type=f32
            )
        if stage == 1:
            total = total + matrix_before_ref[...]
        matrix_ref[...] = total


def pair_call(stage, steps, home, fars, table, left=None, before=None, matrix_before=None):
    count = len(steps)
    feats = 112 if stage == 2 else 128
    vmem = pl.BlockSpec(memory_space=pltpu.VMEM)
    operands = [home, *fars, table]
    if stage == 2:
        operands.append(left)
    if stage > 0:
        operands.append(before)
    if stage == 1:
        operands.append(matrix_before)
    packed = HOMES if stage == 0 else HOMES + 2 * ZC
    scratch = [
        pltpu.VMEM((packed, 48, 2 * SLOTS), bf16),
        pltpu.VMEM((packed, 8, SLOTS), f32),
        pltpu.VMEM((48 * count, SLOTS, SLOTS), bf16),
        pltpu.VMEM((48 * count, feats, SLOTS), bf16),
        pltpu.VMEM((packed, feats, 2 * SLOTS), f32),
    ]
    if stage == 0:
        scratch.append(pltpu.VMEM((HOMES, 72, SLOTS), f32))
    if stage == 1:
        scratch.append(pltpu.VMEM((packed, feats, 2 * SLOTS), f32))
    if stage < 2:
        scratch += [pltpu.VMEM((HOMES, 8, SLOTS), f32)] * 2

    def body(home_ref, *refs):
        far_refs = refs[:count]
        table_ref = refs[count]
        refs = list(refs[count + 1 :])
        left_ref = refs.pop(0) if stage == 2 else far_refs[0]
        before_ref = refs.pop(0) if stage > 0 else None
        matrix_before_ref = refs.pop(0) if stage == 1 else None
        out_ref = refs.pop(0)
        matrix_ref = refs.pop(0) if stage < 2 else None
        main = refs[:5]
        own_ref = refs[5] if stage == 0 else None
        moved_ref = refs[5] if stage == 1 else None
        sums = refs[6:] if stage < 2 else [None] * 2
        pair_body(stage, steps, home_ref, far_refs, left_ref, table_ref, before_ref,
                  matrix_before_ref, out_ref, matrix_ref, *main, own_ref, moved_ref, *sums)

    if stage == 2:
        out = (jax.ShapeDtypeStruct((3, 1, NY, ZC, SLOTS), f32),)
    else:
        out = (
            jax.ShapeDtypeStruct((ZC, NY, 8, SLOTS), f32),
            jax.ShapeDtypeStruct((8, 8), f32),
        )
    return pl.pallas_call(
        body,
        out_shape=out,
        in_specs=[vmem] * len(operands),
        out_specs=(vmem,) * len(out),
        scratch_shapes=scratch,
        compiler_params=pltpu.CompilerParams(vmem_limit_bytes=48 * 2**20),
        name=("pairs_own", "pairs_left", "pairs_rest")[stage],
    )(*operands)


def pack_body(counts_ref, pos_ref, cot_ref, species_ref, out_ref, low_ref, high_ref):
    lane = lax.broadcasted_iota(jnp.int32, (1, SLOTS), 1)
    for y in range(NY):
        for z in range(ZC):
            rows = [pos_ref[k, 0, y, z : z + 1, :] for k in range(3)]
            rows += [cot_ref[k, 0, y, z : z + 1, :] for k in range(3)]
            kind = jnp.where(lane < counts_ref[0, z, y], species_ref[0, y, z : z + 1, :], -1)
            rows += [kind.astype(f32), jnp.zeros((1, SLOTS), f32)]
            packed = jnp.concatenate(rows, axis=0)
            out_ref[z, y] = packed
            if z == 0:
                low_ref[0, y] = packed
            if z == ZC - 1:
                high_ref[0, y] = packed


def pack(counts, positions, cotangent, species):
    vmem = pl.BlockSpec(memory_space=pltpu.VMEM)
    return pl.pallas_call(
        pack_body,
        out_shape=(
            jax.ShapeDtypeStruct((ZC, NY, 8, SLOTS), f32),
            jax.ShapeDtypeStruct((1, NY, 8, SLOTS), f32),
            jax.ShapeDtypeStruct((1, NY, 8, SLOTS), f32),
        ),
        in_specs=[pl.BlockSpec(memory_space=pltpu.SMEM)] + [vmem] * 3,
        out_specs=(vmem,) * 3,
        name="pack",
    )(counts, positions, cotangent, species)


def move(block, dx, dz):
    pairs = []
    for i in range(NX):
        for j in range(NZ):
            pairs.append((i * NZ + j, (i + dx) % NX * NZ + (j + dz) % NZ))
    return lax.ppermute(block, AXES, pairs)


OWN_HALF = [(0, 1, 1), (0, 1, 2), (0, 2, 0), (0, 2, 1), (0, 2, 2)]
OWN_OTHER = [(0, 1, 0), (0, 0, 0), (0, 0, 1), (0, 0, 2)]


def whole(i):
    return [(i, dz, dy) for dz in range(3) for dy in range(3)]


def per_device(positions, cotangent, species, counts, amplitude):
    table = 0.5 * (amplitude + amplitude.T)
    home, low, high = pack(jnp.swapaxes(counts, 1, 2), positions, cotangent, species)
    below = move(high, 0, 1)
    above = move(low, 0, -1)
    column = jnp.concatenate([below, home, above], axis=0)
    left = move(column, 1, 0)
    right = move(column, -1, 0)
    part, matrix = pair_call(0, (0.0,), home, (column,), table)
    part, matrix = pair_call(
        1, (-1.0, 1.0), home, (left, right), table, before=part, matrix_before=matrix
    )
    sent = jnp.broadcast_to(matrix.reshape(1, KINDS * KINDS), (NX * NZ, KINDS * KINDS))
    sent, part = lax.optimization_barrier((sent, part))
    heard = lax.all_to_all(sent, AXES, 0, 0, tiled=True)
    (out,) = pair_call(2, (0.0, 1.0), home, (column, right), table, left=left, before=part)
    heard, out = lax.optimization_barrier((heard, out))
    matrix = jnp.sum(heard, axis=0).reshape(KINDS, KINDS)
    cells_total = NX * NY * NZ * ZC
    total = 6.0 * (matrix + matrix.T)
    return out, step_size * total / (2.0 * math.sqrt(cells_total / SLOTS))


def solution(mesh):
    finer = Mesh(mesh.devices.reshape(2, 8, 2, 2, 4), AXES)
    in_specs = (
        P(None, COL, None, ROW, None),
        P(None, COL, None, ROW, None),
        P(COL, None, ROW, None),
        P(COL, None, ROW),
        P(),
    )
    return jax.shard_map(
        per_device,
        mesh=finer,
        in_specs=in_specs,
        out_specs=(P(None, COL, None, ROW, None), P()),
        check_vma=False,
    )
```

```python
import math

import jax
import jax.numpy as jnp
from jax import lax
from jax.experimental import pallas as pl
from jax.experimental.pallas import tpu as pltpu
from jax.sharding import Mesh
from jax.sharding import PartitionSpec as P

AXES = ("y_hi", "z_ax", "core", "y_lo", "x_ax")
ROW = ("y_lo", "x_ax")
COL = ("y_hi", "z_ax", "core")
NX, NZ = 32, 8
step_size = 0.05
FAR = 1.0e4
NY = 6
ZC = 4
SLOTS = 128
KINDS = 8
SHORT = 32
HOMES = NY * ZC
bf16 = jnp.bfloat16
f32 = jnp.float32


def sublane(shape=(8, SLOTS)):
    return lax.broadcasted_iota(jnp.int32, shape, 0)


def pieces(v):
    high = v.astype(bf16).astype(f32)
    rest = v - high
    mid = rest.astype(bf16).astype(f32)
    return high, mid, rest - mid


def pick(row, lo, hi, value, other):
    return jnp.where((row >= lo) & (row < hi), value, other)


def row_sum(row, lo, hi, value):
    return jnp.sum(pick(row, lo, hi, value, 0.0), axis=0, keepdims=True)


def framed(raw, row, sx, sy, sz):
    shift = jnp.where(row == 0, sx, jnp.where(row == 1, sy, jnp.where(row == 2, sz, 0.0)))
    return raw + shift.astype(f32)


def bead_terms(v, row):
    back = pltpu.roll(v, 3, 0)
    square = row_sum(row, 0, 3, v * v)
    cross = row_sum(row, 3, 6, v * back)
    return back, square, cross


def far_features(v, lhs_ref, feat_ref, slot):
    row = sublane()
    back, square, cross = bead_terms(v, row)
    code = v[6:7]
    ahead = pltpu.roll(v, 5, 0)
    gain = jnp.where(code < 0.0, -FAR, 1.0 - square)
    a = pick(row, 0, 3, ahead, pick(row, 3, 6, back, 0.0))
    ah, am, al = pieces(a)
    qh, qm, ql = pieces(gain)
    rh, rm, rl = pieces(cross)
    one = jnp.where(row == 6, 1.0, 0.0)
    last = row == 7
    lhs = jnp.concatenate(
        [
            jnp.where(last, qh, ah + one),
            jnp.where(last, qm, ah + one),
            jnp.where(last, ql, ah + one),
            jnp.where(last, rh, am),
            jnp.where(last, rm, am),
            jnp.where(last, rl, al),
        ],
        axis=0,
    )
    lhs_ref[slot, :, 0:48] = lhs.astype(bf16).T
    mask = code == row.astype(f32)
    high = v.astype(bf16).astype(f32)
    low = v - high
    rows = [jnp.where(mask, 1.0, 0.0)]
    for part, start in ((high, 0), (low, 0), (high, 3), (low, 3)):
        for k in range(3):
            rows.append(jnp.where(mask, part[start + k : start + k + 1], 0.0))
    if feat_ref.shape[1] == 128:
        rows += [jnp.where(mask, r, 0.0) for r in (rh, rm, rl)]
    else:
        rows.append(jnp.zeros((8, SLOTS), f32))
    feat_ref[slot] = jnp.concatenate(rows, axis=0).astype(bf16)


def home_features(v, gram_ref, frame_ref, h):
    row = sublane()
    back, square, cross = bead_terms(v, row)
    square = jnp.where(v[6:7] < 0.0, FAR, square)
    u = pick(row, 3, 6, 2.0 * back, jnp.where(row == 6, -square, 0.0))
    p = pick(row, 0, 6, -v, jnp.where(row == 6, cross, 0.0))
    last = jnp.where(row == 7, 1.0, 0.0)
    uh, um, ul = pieces(u)
    ph, pm, pl_ = pieces(p)
    gram_ref[h, :, 0:SLOTS] = jnp.concatenate(
        [uh + last, um + last, ul + last, uh, um, uh], axis=0
    ).astype(bf16)
    gram_ref[h, :, SLOTS : 2 * SLOTS] = jnp.concatenate(
        [ph, pm, pl_, ph + last, pm + last, ph + last], axis=0
    ).astype(bf16)
    frame_ref[h] = jnp.where(row == 7, cross, v)


def is_short(ref):
    kinds = ref[0, 0, 6:7]
    for z in range(ref.shape[0]):
        for y in range(NY):
            kinds = jnp.maximum(kinds, ref[z, y, 6:7])
    lane = lax.broadcasted_iota(jnp.int32, (1, SLOTS), 1)
    return jnp.max(jnp.where(lane < SHORT, -1.0, kinds)) < 0.0


def pair_body(stage, steps, home_ref, far_refs, left_ref, table_ref, before_ref,
              matrix_before_ref, out_ref, matrix_ref, gram_ref, frame_ref, lhs_ref, feat_ref,
              acc_ref, own_ref, moved_ref, moment_ref, kind_ref):
    row = sublane()
    lane = lax.broadcasted_iota(jnp.int32, (8, SLOTS), 1)
    quarter = lane // SHORT
    both = jnp.logical_and
    no = jnp.logical_not

    def far_bead(i, z, ye):
        y = lax.rem(ye + 5, 6)
        return framed(
            far_refs[i][z, y], row, steps[i] - 0.5, (ye - 4).astype(f32), (z - 3).astype(f32)
        )

    def home_bead(z, y):
        return framed(home_ref[z, y], row, -0.5, (y - 3).astype(f32), (z - 2).astype(f32))

    def prepare_whole(i, low=0, high=6):
        @pl.loop(8 * low, 8 * high, unroll=8)
        def _(n):
            far_features(far_bead(i, n // 8, n % 8), lhs_ref, feat_ref, i * 48 + n)

    def prepare_short(i):
        @pl.loop(0, 12, unroll=2)
        def _(n):
            v = far_bead(i, n // 2, n % 2 * 4)
            for j in range(1, 4):
                other = pltpu.roll(far_bead(i, n // 2, n % 2 * 4 + j), SHORT * j, 1)
                v = jnp.where(quarter == j, other, v)
            far_features(v, lhs_ref, feat_ref, i * 48 + n // 2 * 8 + n % 2)

    def prepare_home():
        @pl.loop(0, HOMES, unroll=8)
        def _(h):
            home_features(home_bead(h // 6, h % 6), gram_ref, frame_ref, h)

    def prepare_packed():
        @pl.loop(0, 2 * ZC, unroll=2)
        def _(n):
            z = n // 2
            y = n % 2 * 3
            v = home_bead(z, y)
            for j in (1, 2):
                v = jnp.where(quarter == j, pltpu.roll(home_bead(z, y + j), SHORT * j, 1), v)
            v = jnp.where(quarter == 3, jnp.where(row == 6, -1.0, 0.0), v)
            home_features(v, gram_ref, frame_ref, HOMES + n)

    def gather(h, slots, target_ref):
        gram = gram_ref[h]
        acc = None
        for slot in slots:
            g = jnp.dot(lhs_ref[slot, :, 0:48], gram, preferred_element_type=f32)
            e = jnp.maximum(g[:, :SLOTS], 0.0)
            terms = jnp.concatenate([e * e, e * g[:, SLOTS:]], axis=1)
            high = terms.astype(bf16)
            low = (terms - high.astype(f32)).astype(bf16)
            feat = feat_ref[slot]
            part = jnp.dot(
                jnp.concatenate([feat, feat], axis=1),
                jnp.concatenate([high, low], axis=0),
                preferred_element_type=f32,
            )
            if stage == 0 and acc is None:
                own_ref[h] = part[56:, :SLOTS]
            acc = part if acc is None else acc + part
        target_ref[h] = acc

    def gather_homes(group, tiles, target_ref, first=0, last=HOMES):
        @pl.loop(0, (last - first) // group)
        def _(q):
            for j in range(group):
                h = first + q * group + j
                z = h // 6
                y = h % 6
                gather(h, [(i * 6 + z + dz) * 8 + y + dy for i, dz, dy in tiles], target_ref)

    def gather_short(i, tiles):
        @pl.loop(0, ZC)
        def _(z):
            for y in range(NY):
                slots = [(z + dz) * 8 + y + dy for _, dz, dy in tiles]
                for dz in range(3):
                    for half in range(y // 4, (y + 2) // 4 + 1):
                        slots.append((i * 6 + z + dz) * 8 + half)
                gather(z * 6 + y, slots, acc_ref)

    def gather_packed(i, short, depths, target_ref):
        @pl.loop(0, ZC // 2)
        def _(pair):
            for z in (2 * pair, 2 * pair + 1):
                for t in range(2):
                    cells = range(2) if short else range(3 * t, 3 * t + 5)
                    slots = [(i * 6 + z + dz) * 8 + c for dz in depths for c in cells]
                    gather(HOMES + 2 * z + t, slots, target_ref)

    if stage == 0:
        prepare_whole(0, 1, 6)
        prepare_home()
        gather_homes(8, OWN_HALF, acc_ref)
    else:
        home_short = is_short(home_ref)
        left_short = is_short(left_ref)
        right_short = is_short(far_refs[1])
        moves = both(both(no(home_short), left_short), no(right_short))
        packed_moves = both(home_short, no(right_short))
        pl.when(home_short)(prepare_packed)
    if stage == 1:
        pl.when(left_short)(lambda: prepare_short(0))
        pl.when(no(left_short))(lambda: prepare_whole(0))
        pl.when(moves)(lambda: prepare_whole(1, 0, 4))
        pl.when(packed_moves)(lambda: prepare_whole(1, 0, 5))
        pl.when(no(home_short))(prepare_home)
        pl.when(both(home_short, left_short))(lambda: gather_packed(0, True, range(3), acc_ref))
        pl.when(both(home_short, no(left_short)))(lambda: gather_packed(0, False, range(3), acc_ref))
        pl.when(both(no(home_short), left_short))(lambda: gather_short(0, []))
        pl.when(both(no(home_short), no(left_short)))(lambda: gather_homes(6, whole(0), acc_ref))
        pl.when(moves)(lambda: gather_homes(6, whole(1), moved_ref, 0, HOMES // 2))
        pl.when(packed_moves)(lambda: gather_packed(1, False, (0, 1), moved_ref))
        moment_ref[...] = jnp.zeros_like(moment_ref)
        kind_ref[...] = jnp.zeros_like(kind_ref)
    if stage == 2:
        prepare_whole(0, 0, 5)
        pl.when(right_short)(lambda: prepare_short(1))
        partly = jnp.logical_or(moves, packed_moves)
        pl.when(partly)(lambda: prepare_whole(1, 2, 6))
        pl.when(no(jnp.logical_or(partly, right_short)))(lambda: prepare_whole(1))
        prepare_home()
        pl.when(home_short)(lambda: gather_homes(6, OWN_OTHER, acc_ref))
        pl.when(both(home_short, right_short))(lambda: gather_packed(1, True, range(3), acc_ref))
        pl.when(packed_moves)(lambda: gather_packed(1, False, (2,), acc_ref))
        pl.when(both(no(home_short), right_short))(lambda: gather_short(1, OWN_OTHER))

        @pl.when(moves)
        def _():
            gather_homes(6, OWN_OTHER, acc_ref, 0, HOMES // 2)
            gather_homes(4, OWN_OTHER + whole(1), acc_ref, HOMES // 2)

        pl.when(both(both(no(home_short), no(left_short)), no(right_short)))(
            lambda: gather_homes(4, OWN_OTHER + whole(1), acc_ref)
        )

    table = table_ref[...]
    columns = [jnp.broadcast_to(table[:, s : s + 1], (8, SLOTS)) for s in range(KINDS)]

    def finish(h, m, moved):
        v = frame_ref[h]
        code = v[6:7]
        mix = jnp.zeros((8, SLOTS), f32)
        for s in range(KINDS):
            mix = jnp.where(code == float(s), columns[s], mix)

        def part(f, half):
            return acc_ref[h, 8 * f : 8 * f + 8, half * SLOTS : (half + 1) * SLOTS]

        def every(f, half):
            value = part(f, half)
            if moved:
                value = value + moved_ref[h, 8 * f : 8 * f + 8, half * SLOTS : (half + 1) * SLOTS]
            return value

        def mixed(value):
            return jnp.sum(value * mix, axis=0, keepdims=True)

        def away(f):
            if stage == 0:
                return part(f, 0) - own_ref[h, 8 * f - 56 : 8 * f - 48]
            return part(f, 0)

        c1 = mixed(every(0, 0))
        c2 = mixed(every(0, 1))
        rows = []
        for k in range(3):
            stretch = v[3 + k : 4 + k] * c1 - mixed(every(7 + k, 0) + every(10 + k, 0))
            bend = v[k : k + 1] * c2 - mixed(every(1 + k, 1) + every(4 + k, 1))
            rows.append(step_size * (6.0 * stretch - 24.0 * bend))
        if stage < 2:
            moment = v[7:8] * part(0, 0) + (away(13) + away(14) + away(15))
            for k in range(3):
                moment = moment - v[3 + k : 4 + k] * (part(1 + k, 0) + part(4 + k, 0))
                moment = moment - v[k : k + 1] * (away(7 + k) + away(10 + k))
            moment_ref[m] = moment
            kind_ref[m] = jnp.where(code == row.astype(f32), 1.0, 0.0)
        return rows

    def finish_homes(moved, first=0, last=HOMES):
        @pl.loop(first, last, unroll=6)
        def _(h):
            z = h // 6
            y = h % 6
            rows = finish(h, h, moved)
            for k in range(3):
                if stage == 2:
                    out_ref[k, 0, y, pl.ds(z, 1), :] = rows[k] + before_ref[z, y, k : k + 1]
                else:
                    old = frame_ref[h, 3 + k : 4 + k] if stage == 0 else before_ref[z, y, k : k + 1]
                    out_ref[z, y, k : k + 1] = rows[k] + old

    def finish_packed(moved):
        @pl.loop(0, ZC, unroll=2)
        def _(z):
            for t in range(2):
                rows = finish(HOMES + 2 * z + t, 2 * z + t, moved)
                for j in range(3):
                    y = 3 * t + j
                    for k in range(3):
                        value = pltpu.roll(rows[k], (SLOTS - SHORT * j) % SLOTS, 1) if j else rows[k]
                        value = jnp.where(lane[0:1] < SHORT, value, 0.0)
                        if stage == 2:
                            out_ref[k, 0, y, pl.ds(z, 1), :] += value
                        else:
                            out_ref[z, y, k : k + 1] = before_ref[z, y, k : k + 1] + value

    if stage == 0:
        finish_homes(False)
    elif stage == 1:
        pl.when(moves)(lambda: finish_homes(True, 0, HOMES // 2))
        pl.when(moves)(lambda: finish_homes(False, HOMES // 2))
        pl.when(both(no(home_short), no(moves)))(lambda: finish_homes(False))
        pl.when(packed_moves)(lambda: finish_packed(True))
        pl.when(both(home_short, right_short))(lambda: finish_packed(False))
    else:
        finish_homes(False)
        pl.when(home_short)(lambda: finish_packed(False))

    if stage < 2:
        total = jnp.zeros((8, 8), f32)
        moments = jnp.concatenate([moment_ref[h] for h in range(HOMES)], axis=1)
        kinds = jnp.concatenate([kind_ref[h] for h in range(HOMES)], axis=1).astype(bf16)
        for piece in pieces(moments):
            total = total + lax.dot_general(
                piece.astype(bf16), kinds, (((1,), (1,)), ((), ())), preferred_element_type=f32
            )
        if stage == 1:
            total = total + matrix_before_ref[...]
        matrix_ref[...] = total


def pair_call(stage, steps, home, fars, table, left=None, before=None, matrix_before=None):
    count = len(steps)
    feats = 112 if stage == 2 else 128
    vmem = pl.BlockSpec(memory_space=pltpu.VMEM)
    operands = [home, *fars, table]
    if stage == 2:
        operands.append(left)
    if stage > 0:
        operands.append(before)
    if stage == 1:
        operands.append(matrix_before)
    packed = HOMES if stage == 0 else HOMES + 2 * ZC
    scratch = [
        pltpu.VMEM((packed, 48, 2 * SLOTS), bf16),
        pltpu.VMEM((packed, 8, SLOTS), f32),
        pltpu.VMEM((48 * count, SLOTS, SLOTS), bf16),
        pltpu.VMEM((48 * count, feats, SLOTS), bf16),
        pltpu.VMEM((packed, feats, 2 * SLOTS), f32),
    ]
    if stage == 0:
        scratch.append(pltpu.VMEM((HOMES, 72, SLOTS), f32))
    if stage == 1:
        scratch.append(pltpu.VMEM((packed, feats, 2 * SLOTS), f32))
    if stage < 2:
        scratch += [pltpu.VMEM((HOMES, 8, SLOTS), f32)] * 2

    def body(home_ref, *refs):
        far_refs = refs[:count]
        table_ref = refs[count]
        refs = list(refs[count + 1 :])
        left_ref = refs.pop(0) if stage == 2 else far_refs[0]
        before_ref = refs.pop(0) if stage > 0 else None
        matrix_before_ref = refs.pop(0) if stage == 1 else None
        out_ref = refs.pop(0)
        matrix_ref = refs.pop(0) if stage < 2 else None
        main = refs[:5]
        own_ref = refs[5] if stage == 0 else None
        moved_ref = refs[5] if stage == 1 else None
        sums = refs[6:] if stage < 2 else [None] * 2
        pair_body(stage, steps, home_ref, far_refs, left_ref, table_ref, before_ref,
                  matrix_before_ref, out_ref, matrix_ref, *main, own_ref, moved_ref, *sums)

    if stage == 2:
        out = (jax.ShapeDtypeStruct((3, 1, NY, ZC, SLOTS), f32),)
    else:
        out = (
            jax.ShapeDtypeStruct((ZC, NY, 8, SLOTS), f32),
            jax.ShapeDtypeStruct((8, 8), f32),
        )
    return pl.pallas_call(
        body,
        out_shape=out,
        in_specs=[vmem] * len(operands),
        out_specs=(vmem,) * len(out),
        scratch_shapes=scratch,
        compiler_params=pltpu.CompilerParams(vmem_limit_bytes=48 * 2**20),
        name=("pairs_own", "pairs_left", "pairs_rest")[stage],
    )(*operands)


def pack_body(counts_ref, pos_ref, cot_ref, species_ref, out_ref, low_ref, high_ref):
    lane = lax.broadcasted_iota(jnp.int32, (1, SLOTS), 1)
    for y in range(NY):
        for z in range(ZC):
            rows = [pos_ref[k, 0, y, z : z + 1, :] for k in range(3)]
            rows += [cot_ref[k, 0, y, z : z + 1, :] for k in range(3)]
            kind = jnp.where(lane < counts_ref[0, z, y], species_ref[0, y, z : z + 1, :], -1)
            rows += [kind.astype(f32), jnp.zeros((1, SLOTS), f32)]
            packed = jnp.concatenate(rows, axis=0)
            out_ref[z, y] = packed
            if z == 0:
                low_ref[0, y] = packed
            if z == ZC - 1:
                high_ref[0, y] = packed


def pack(counts, positions, cotangent, species):
    vmem = pl.BlockSpec(memory_space=pltpu.VMEM)
    return pl.pallas_call(
        pack_body,
        out_shape=(
            jax.ShapeDtypeStruct((ZC, NY, 8, SLOTS), f32),
            jax.ShapeDtypeStruct((1, NY, 8, SLOTS), f32),
            jax.ShapeDtypeStruct((1, NY, 8, SLOTS), f32),
        ),
        in_specs=[pl.BlockSpec(memory_space=pltpu.SMEM)] + [vmem] * 3,
        out_specs=(vmem,) * 3,
        name="pack",
    )(counts, positions, cotangent, species)


def move(block, dx, dz):
    pairs = []
    for i in range(NX):
        for j in range(NZ):
            pairs.append((i * NZ + j, (i + dx) % NX * NZ + (j + dz) % NZ))
    return lax.ppermute(block, AXES, pairs)


OWN_HALF = [(0, 1, 1), (0, 1, 2), (0, 2, 0), (0, 2, 1), (0, 2, 2)]
OWN_OTHER = [(0, 1, 0), (0, 0, 0), (0, 0, 1), (0, 0, 2)]


def whole(i):
    return [(i, dz, dy) for dz in range(3) for dy in range(3)]


def per_device(positions, cotangent, species, counts, amplitude):
    table = 0.5 * (amplitude + amplitude.T)
    home, low, high = pack(jnp.swapaxes(counts, 1, 2), positions, cotangent, species)
    below = move(high, 0, 1)
    above = move(low, 0, -1)
    column = jnp.concatenate([below, home, above], axis=0)
    left = move(column, 1, 0)
    right = move(column, -1, 0)
    part, matrix = pair_call(0, (0.0,), home, (column,), table)
    part, matrix = pair_call(
        1, (-1.0, 1.0), home, (left, right), table, before=part, matrix_before=matrix
    )
    sent = jnp.broadcast_to(matrix.reshape(1, KINDS * KINDS), (NX * NZ, KINDS * KINDS))
    sent, part = lax.optimization_barrier((sent, part))
    heard = lax.all_to_all(sent, AXES, 0, 0, tiled=True)
    (out,) = pair_call(2, (0.0, 1.0), home, (column, right), table, left=left, before=part)
    heard, out = lax.optimization_barrier((heard, out))
    matrix = jnp.sum(heard, axis=0).reshape(KINDS, KINDS)
    cells_total = NX * NY * NZ * ZC
    total = 6.0 * (matrix + matrix.T)
    return out, step_size * total / (2.0 * math.sqrt(cells_total / SLOTS))


def solution(mesh):
    finer = Mesh(mesh.devices.reshape(2, 8, 2, 2, 4), AXES)
    in_specs = (
        P(None, COL, None, ROW, None),
        P(None, COL, None, ROW, None),
        P(COL, None, ROW, None),
        P(COL, None, ROW),
        P(),
    )
    return jax.shard_map(
        per_device,
        mesh=finer,
        in_specs=in_specs,
        out_specs=(P(None, COL, None, ROW, None), P()),
        check_vma=False,
    )
```
